32 devices in a mesh: strip: 2 (over x), swath: 8 (over z, y), group: 2 (over core).
Axes of the slice: x: 2, y: 2, z: 4, core: 2. Of those that a mesh axis runs over, the one named last changes fastest.
Arguments:
- tokens_b: bfloat16 [256, 256, 384], P(('strip', 'swath'), 'group'), parts along dimension 0
- tokens_a: bfloat16 [256, 256, 384], P(('strip', 'swath'), 'group'), parts along dimension 0
- pack_rows: int32 [16, 2, 16, 1024], P(('strip', 'swath'), 'group'), parts along dimension 0, may hold values from 0 to 2047, as said below
- pack_count: int32 [16, 2, 16], P(('strip', 'swath'), 'group'), parts along dimension 0, may hold values from 0 to 1024, as said below
- gather_slots: int32 [4, 256, 256], P(None, ('strip', 'swath'), 'group'), parts along dimension 1, may hold values from 0 to 16383, as said below
- blend_weights: float32 [4, 256, 256], P(None, ('strip', 'swath'), 'group'), parts along dimension 1, may hold values from 0 to 1
- swath_gain: float32 [384], replicated, may hold values from 0.5 to 1.5
- swath_query: bfloat16 [384, 384], replicated
- swath_key: bfloat16 [384, 384], replicated
- swath_value: bfloat16 [384, 384], replicated, may hold values from -0.3125 to 0.3125
- swath_out: bfloat16 [384, 384], replicated, may hold values from -0.3125 to 0.3125
- query_gain: float32 [384], replicated, may hold values from 0.5 to 1.5
- source_gain: float32 [384], replicated, may hold values from 0.5 to 1.5
- cross_query: bfloat16 [384, 384], replicated
- cross_key: bfloat16 [384, 384], replicated
- cross_value: bfloat16 [384, 384], replicated, may hold values from -0.3125 to 0.3125
- cross_out: bfloat16 [384, 384], replicated, may hold values from -0.3125 to 0.3125
- conv_gain: float32 [384], replicated, may hold values from 0.5 to 1.5
- conv_first: bfloat16 [3, 3, 384, 384], replicated, may hold values from -0.109375 to 0.109375
- conv_second: bfloat16 [3, 3, 384, 384], replicated, may hold values from -0.109375 to 0.109375
Outputs:
- merged: bfloat16 [256, 256, 384], P(('strip', 'swath'), 'group'), parts along dimension 0
The draws below stay inside these ranges and needn't reach their ends.
There are 2 independent parts, one for each index of `strip`. The reference program is written for one: setup_inputs(seed, part) draws one part's arguments, and reference() takes and returns one part's arrays. A program takes and returns all parts, laid end to end along the dimension named above; an argument that names none is the same for every part. Nothing has to cross between parts.
Inputs may be any that keep to these rules, and one draw needn't show every extreme that they name: `pack_rows`: entry [s, g, e, c] is a cell of device (s, g)'s block; the first pack_count[s, g, e] entries of a block are distinct. `pack_count`: zero unless the destination device's swath index differs from the source's by at most one; every destination receives exactly 1024 live rows from one of its sources. `gather_slots`: entry [k, i, j] is p * 1024 + c with p a source device whose swath index differs from that of the device holding cell (i, j) by at most one.
All inputs are finite; a program needn't handle non-finite values.
Results may differ from the reference program's by a relative error of at most 0.0095.
Values may be sent and summed in bfloat16 or wider, within the bound.
No kernel may reach another device: no remote copies, remote signals or barrier semaphores. Data moves between devices by JAX's collectives and lax.ppermute only.
A program may use at most 128 MiB of HBM per device.

```python
import jax
import jax.numpy as jnp
from jax import lax

C = 384
HEADS = 6
HD = 64
ROWS_DEV = 16
COLS_DEV = 128
TILE_R = 16
TILE_C = 16
TOK_DEV = 2048
CAP = 1024
PEERS = 16
HB = 128
WB = 256
N_SWATH = 8
N_GROUP = 2


def route_tables(key):
    base = jax.random.fold_in(key, 101)
    source_swath = jnp.arange(N_SWATH, dtype=jnp.int32)[:, None, None]
    source_group = jnp.arange(N_GROUP, dtype=jnp.int32)[None, :, None]
    dest_peer = jnp.arange(PEERS, dtype=jnp.int32)
    dest_swath = (dest_peer // N_GROUP)[None, None, :]
    nearby = jnp.abs(source_swath - dest_swath) <= 1
    counts = jax.random.randint(jax.random.fold_in(base, 1), (N_SWATH, N_GROUP, PEERS), CAP // 4, CAP + 1)
    chosen_step = jax.random.randint(jax.random.fold_in(base, 2), (PEERS,), -1, 2)
    chosen_swath = jnp.clip(dest_peer // N_GROUP + chosen_step, 0, N_SWATH - 1)
    chosen_group = jax.random.randint(jax.random.fold_in(base, 3), (PEERS,), 0, N_GROUP)
    filled = (source_swath == chosen_swath[None, None, :]) & (source_group == chosen_group[None, None, :])
    counts = jnp.where(filled, CAP, counts)
    counts = jnp.where(nearby, counts, 0).astype(jnp.int32)
    upper_key = max(2 ** 30 // TOK_DEV, 1)
    order_keys = jax.random.randint(jax.random.fold_in(base, 4), (N_SWATH, N_GROUP, PEERS, TOK_DEV), 0, upper_key) * TOK_DEV + jnp.arange(TOK_DEV, dtype=jnp.int32)
    rows_chosen = jnp.argsort(order_keys, axis=-1)[..., :CAP].astype(jnp.int32)
    return (rows_chosen, counts)


def draw_pack_rows(key, part):
    return route_tables(key)[0]


def draw_pack_count(key, part):
    return route_tables(key)[1]


def draw_gather_slots(key, part):
    rows_chosen, counts = route_tables(key)
    base = jax.random.fold_in(key, 202)
    cell_row = jnp.arange(HB, dtype=jnp.int32)[:, None]
    cell_col = jnp.arange(WB, dtype=jnp.int32)[None, :]
    dest_swath = jnp.broadcast_to(cell_row // ROWS_DEV, (HB, WB))
    dest_peer = dest_swath * N_GROUP + cell_col // COLS_DEV
    step_pick = jax.random.randint(jax.random.fold_in(base, 1), (4, HB, WB), -1, 2)
    source_swath = jnp.clip(dest_swath[None] + step_pick, 0, N_SWATH - 1)
    source_group = jax.random.randint(jax.random.fold_in(base, 2), (4, HB, WB), 0, N_GROUP)
    live_count = counts[source_swath, source_group, jnp.broadcast_to(dest_peer[None], (4, HB, WB))]
    upper = jnp.minimum(live_count + CAP // 8, CAP)
    slot_place = jax.random.randint(jax.random.fold_in(base, 3), (4, HB, WB), 0, upper)
    return ((source_swath * N_GROUP + source_group) * CAP + slot_place).astype(jnp.int32)


def token_field(key, salt):
    own_key = jax.random.fold_in(key, salt)
    noise = jax.random.normal(own_key, (HB, WB, C), jnp.float32)
    return jnp.clip(noise, -8.0, 8.0).astype(jnp.bfloat16)


def draw_tokens_b(key, part):
    return token_field(key, 21)


def draw_tokens_a(key, part):
    return token_field(key, 22)


def paired_weights(key, salt):
    own_key = jax.random.fold_in(key, salt)
    first = jax.random.normal(jax.random.fold_in(own_key, 1), (C, C), jnp.float32) * C ** (-0.5)
    second = jax.random.normal(jax.random.fold_in(own_key, 2), (C, C), jnp.float32) * C ** (-0.5)
    return (first.astype(jnp.bfloat16), second.astype(jnp.bfloat16))


def draw_swath_query(key, part):
    return paired_weights(key, 31)[0]


def draw_swath_key(key, part):
    return paired_weights(key, 31)[1]


def draw_cross_query(key, part):
    return paired_weights(key, 41)[0]


def draw_cross_key(key, part):
    return paired_weights(key, 41)[1]


def block_scale(stream_key, extent, shards, smallest, top_value):
    gain, own = 1.0, jax.random.fold_in(stream_key, 6)
    for dim, parts in shards:
        heights = jnp.exp(jax.random.uniform(jax.random.fold_in(own, dim), (parts,), jnp.float32, smallest / len(shards), top_value / len(shards)))
        gain = gain * jnp.repeat(heights, extent[dim] // parts).reshape([-1 if axis == dim else 1 for axis in range(len(extent))])
    return gain


def scatter_about(stream_key, shape, width, limit, kind=jnp.bfloat16):
    entries = jax.random.normal(stream_key, shape, jnp.float32) * width
    return jnp.minimum(jnp.maximum(entries, -limit), limit).astype(kind)


def setup_inputs(seed: int = 0, part: int = 0) -> dict:
    splits = jax.random.split(jax.random.key(seed), 21)
    part_splits = jax.random.split(jax.random.fold_in(splits[20], part), 21)
    return {
        "tokens_b": draw_tokens_b(jax.random.fold_in(jax.random.fold_in(splits[20], part), 71), part),
        "tokens_a": draw_tokens_a(jax.random.fold_in(jax.random.fold_in(splits[20], part), 71), part),
        "pack_rows": draw_pack_rows(jax.random.fold_in(jax.random.fold_in(splits[20], part), 71), part),
        "pack_count": draw_pack_count(jax.random.fold_in(jax.random.fold_in(splits[20], part), 71), part),
        "gather_slots": draw_gather_slots(jax.random.fold_in(jax.random.fold_in(splits[20], part), 71), part),
        "blend_weights": jnp.clip(1.0 * jax.random.uniform(part_splits[5], (4, HB, WB), jnp.float32) ** block_scale(part_splits[5], (4, HB, WB), ((1, 8), (2, 2)), -0.2, 0.2), 0.0, 1.0),
        "swath_gain": jnp.clip(1.0 + 0.1 * jax.random.normal(splits[6], (C,), jnp.float32), 0.5, 1.5),
        "swath_query": draw_swath_query(jax.random.fold_in(splits[20], 71), part),
        "swath_key": draw_swath_key(jax.random.fold_in(splits[20], 71), part),
        "swath_value": scatter_about(splits[9], (C, C), C ** -0.5, 0.3125),
        "swath_out": scatter_about(splits[10], (C, C), C ** -0.5, 0.3125),
        "query_gain": jnp.clip(1.0 + 0.1 * jax.random.normal(splits[11], (C,), jnp.float32), 0.5, 1.5),
        "source_gain": jnp.clip(1.0 + 0.1 * jax.random.normal(splits[12], (C,), jnp.float32), 0.5, 1.5),
        "cross_query": draw_cross_query(jax.random.fold_in(splits[20], 71), part),
        "cross_key": draw_cross_key(jax.random.fold_in(splits[20], 71), part),
        "cross_value": scatter_about(splits[15], (C, C), C ** -0.5, 0.3125),
        "cross_out": scatter_about(splits[16], (C, C), C ** -0.5, 0.3125),
        "conv_gain": jnp.clip(1.0 + 0.1 * jax.random.normal(splits[17], (C,), jnp.float32), 0.5, 1.5),
        "conv_first": scatter_about(splits[18], (3, 3, C, C), (9 * C) ** -0.5, 0.109375),
        "conv_second": scatter_about(splits[19], (3, 3, C, C), (9 * C) ** -0.5, 0.109375),
    }


EPSILON = 1e-06

def rms_gain(values, gain_vector):
    widened = values.astype(jnp.float32)
    inverse = lax.rsqrt(lax.optimization_barrier(jnp.mean(widened * widened, axis=-1, keepdims=True)) + EPSILON)
    return (widened * inverse * gain_vector).astype(jnp.bfloat16)

def project(values, matrix):
    flattened = values.reshape(-1, values.shape[-1])
    result = jnp.dot(flattened, matrix, preferred_element_type=jnp.float32)
    return result.reshape(values.shape[:-1] + (matrix.shape[-1],))

def window_attend(query_field, key_field, value_field, live_mask):
    height, breadth, channels = query_field.shape
    query_wide = query_field.astype(jnp.float32)
    score_scale = HD ** (-0.5)
    score_list = []
    for row_step in range(7):
        for col_step in range(7):
            key_part = key_field[row_step:row_step + height, col_step:col_step + breadth].astype(jnp.float32)
            head_score = (query_wide * key_part).reshape(height, breadth, HEADS, HD).sum(-1) * score_scale
            allowed = live_mask[row_step:row_step + height, col_step:col_step + breadth]
            score_list.append(jnp.where(allowed[:, :, None], head_score, -jnp.inf))
    scores = jnp.stack(score_list)
    row_peak = lax.optimization_barrier(jnp.max(scores, axis=0))
    raised = jnp.exp(scores - row_peak[None])
    attn_weights = (raised / lax.optimization_barrier(jnp.sum(raised, axis=0))[None]).astype(jnp.bfloat16)
    accumulated = jnp.zeros((height, breadth, channels), jnp.float32)
    offset_index = 0
    for row_step in range(7):
        for col_step in range(7):
            spread = jnp.repeat(attn_weights[offset_index].astype(jnp.float32), HD, axis=-1)
            value_part = value_field[row_step:row_step + height, col_step:col_step + breadth].astype(jnp.float32)
            accumulated = accumulated + spread * value_part
            offset_index += 1
    return accumulated.astype(jnp.bfloat16)

def neighbour_layer(tokens, gain_vector, w_query, w_key, w_value, w_output):
    normed = rms_gain(tokens, gain_vector)
    query_field = project(normed, w_query).astype(jnp.bfloat16)
    key_field = project(normed, w_key).astype(jnp.bfloat16)
    value_field = project(normed, w_value).astype(jnp.bfloat16)
    padding = ((3, 3), (3, 3), (0, 0))
    live_mask = jnp.pad(jnp.ones(tokens.shape[:2], jnp.int32), 3) > 0
    window_mix = window_attend(query_field, jnp.pad(key_field, padding), jnp.pad(value_field, padding), live_mask)
    return (tokens.astype(jnp.float32) + project(window_mix, w_output)).astype(jnp.bfloat16)

def regrid(shifted, pack_rows, pack_count, gather_slots, blend_weights):
    cell_row = jnp.arange(HB, dtype=jnp.int32)[:, None]
    cell_col = jnp.arange(WB, dtype=jnp.int32)[None, :]
    dest_peer = jnp.broadcast_to(cell_row // ROWS_DEV * N_GROUP + cell_col // COLS_DEV, (HB, WB))
    accumulated = jnp.zeros((HB, WB, C), jnp.float32)
    for ref_step in range(4):
        slot_value = gather_slots[ref_step]
        source_peer = slot_value // CAP
        slot_place = slot_value % CAP
        source_swath = source_peer // N_GROUP
        source_group = source_peer % N_GROUP
        cell_index = pack_rows[source_swath, source_group, dest_peer, slot_place]
        live_ref = slot_place < pack_count[source_swath, source_group, dest_peer]
        picked = shifted[source_swath * ROWS_DEV + cell_index // COLS_DEV, source_group * COLS_DEV + cell_index % COLS_DEV]
        term = blend_weights[ref_step][:, :, None] * picked.astype(jnp.float32)
        accumulated = accumulated + jnp.where(live_ref[:, :, None], term, 0.0)
    return accumulated.astype(jnp.bfloat16)

def to_tiles(field):
    height, breadth, channels = field.shape
    shaped = field.reshape(height // TILE_R, TILE_R, breadth // TILE_C, TILE_C, channels)
    return shaped.transpose(0, 2, 1, 3, 4).reshape(-1, TILE_R * TILE_C, channels)

def from_tiles(tiles, height, breadth):
    channels = tiles.shape[-1]
    shaped = tiles.reshape(height // TILE_R, breadth // TILE_C, TILE_R, TILE_C, channels)
    return shaped.transpose(0, 2, 1, 3, 4).reshape(height, breadth, channels)

def tile_attend(query_field, key_field, value_field):
    height, breadth, channels = query_field.shape
    length = TILE_R * TILE_C
    query_tiles = to_tiles(query_field).reshape(-1, length, HEADS, HD).astype(jnp.float32)
    key_tiles = to_tiles(key_field).reshape(-1, length, HEADS, HD).astype(jnp.float32)
    value_tiles = to_tiles(value_field).reshape(-1, length, HEADS, HD).astype(jnp.float32)
    scores = jnp.einsum('tlhd,tmhd->thlm', query_tiles, key_tiles) * HD ** (-0.5)
    row_peak = lax.optimization_barrier(jnp.max(scores, axis=-1, keepdims=True))
    raised = jnp.exp(scores - row_peak)
    attn_weights = (raised / lax.optimization_barrier(jnp.sum(raised, axis=-1, keepdims=True))).astype(jnp.bfloat16)
    tile_mix = jnp.einsum('thlm,tmhd->tlhd', attn_weights.astype(jnp.float32), value_tiles).astype(jnp.bfloat16)
    return from_tiles(tile_mix.reshape(-1, length, channels), height, breadth)

def conv_valid(padded, kernel):
    height = padded.shape[0] - 2
    breadth = padded.shape[1] - 2
    accumulated = jnp.zeros((height, breadth, kernel.shape[-1]), jnp.float32)
    for row_step in range(3):
        for col_step in range(3):
            accumulated = accumulated + project(padded[row_step:row_step + height, col_step:col_step + breadth], kernel[row_step, col_step])
    return accumulated

def reference(tokens_b, tokens_a, pack_rows, pack_count, gather_slots, blend_weights, swath_gain, swath_query, swath_key, swath_value, swath_out, query_gain, source_gain, cross_query, cross_key, cross_value, cross_out, conv_gain, conv_first, conv_second):
    shifted = neighbour_layer(tokens_b, swath_gain, swath_query, swath_key, swath_value, swath_out)
    resampled = regrid(shifted, pack_rows, pack_count, gather_slots, blend_weights)
    normed_a = rms_gain(tokens_a, query_gain)
    normed_r = rms_gain(resampled, source_gain)
    query_a = project(normed_a, cross_query).astype(jnp.bfloat16)
    key_r = project(normed_r, cross_key).astype(jnp.bfloat16)
    value_r = project(normed_r, cross_value).astype(jnp.bfloat16)
    tile_mix = tile_attend(query_a, key_r, value_r)
    joined = (tokens_a.astype(jnp.float32) + project(tile_mix, cross_out)).astype(jnp.bfloat16)
    normed_c = rms_gain(joined, conv_gain)
    padding = ((1, 1), (1, 1), (0, 0))
    inner_field = jax.nn.gelu(conv_valid(jnp.pad(normed_c, padding), conv_first), approximate=True).astype(jnp.bfloat16)
    second = conv_valid(jnp.pad(inner_field, padding), conv_second)
    return (joined.astype(jnp.float32) + second).astype(jnp.bfloat16)
```

```python
import functools

import jax
import jax.numpy as jnp
import numpy as np
from jax import lax
from jax.experimental import pallas as pl
from jax.experimental.pallas import tpu as pltpu
from jax.sharding import PartitionSpec as P


EPSILON = 1e-06
ROWS = 4
SPAN = ROWS + 6
QC = 16
KC = 24

def rms_rows(x, gain):
    inv = lax.rsqrt(jnp.mean(x * x, axis=-1, keepdims=True) + EPSILON)
    return x * inv * gain

def window_kernel(plan, place_ref, inside_ref, keyrow_ref, keycol_ref, gain_ref, wq_ref, wk_ref, wv_ref, wo_ref,
                  *rest):
    n_src = len(plan)
    srcs, edges = rest[:n_src], rest[n_src:2 * n_src]
    out_ref, tok, side, normed, qs, kv, mix, sems = rest[2 * n_src:]
    breadth = tok.shape[1]
    channels = tok.shape[2]
    wide = normed.shape[1]
    copies = []
    for n, (dst0, src0, count) in enumerate(plan):
        copies.append(pltpu.make_async_copy(srcs[n].at[pl.ds(src0, count)], tok.at[pl.ds(dst0, count)], sems.at[2 * n]))
        copies.append(pltpu.make_async_copy(edges[n].at[pl.ds(src0, count)], side.at[pl.ds(dst0, count)], sems.at[2 * n + 1]))
    for c in copies:
        c.start()
    gain = gain_ref[...]
    normed[:, breadth:, :] = jnp.zeros((SPAN, wide - breadth, channels), jnp.float32)
    for c in copies:
        c.wait()
    for r in range(SPAN):
        x = rms_rows(tok[r].astype(jnp.float32), gain)
        normed[r, 3:3 + breadth, :] = x
        if 3 <= r < 3 + ROWS:
            qs[r - 3] = x.astype(jnp.bfloat16)
        x = rms_rows(side[r].astype(jnp.float32), gain)
        normed[r, 0:3, :] = x[5:8]
        normed[r, 3 + breadth:6 + breadth, :] = x[0:3]
    q = jnp.dot(qs[...].reshape(ROWS * breadth, channels), wq_ref[...], preferred_element_type=jnp.float32)
    qs[...] = (q.astype(jnp.bfloat16) * jnp.bfloat16(0.125)).reshape(ROWS, breadth, channels)
    flat = normed[...].reshape(SPAN * wide, channels).astype(jnp.bfloat16)
    kv[:, :, :channels] = jnp.dot(flat, wk_ref[...], preferred_element_type=jnp.float32).reshape(SPAN, wide, channels)
    kv[:, :, channels:] = jnp.dot(flat, wv_ref[...], preferred_element_type=jnp.float32).reshape(SPAN, wide, channels)
    row0, col0, height, width = place_ref[0], place_ref[1], place_ref[2], place_ref[3]
    krow = keyrow_ref[...] + row0
    row_ok = (krow >= 0) & (krow < height)
    low = lax.broadcasted_iota(jnp.int32, (ROWS * QC, 128), 1) < 64
    ones = jnp.ones((SPAN * KC, 128), jnp.bfloat16)

    def block(cb, carry):
        c0 = pl.multiple_of(cb * QC, QC)
        kcol = keycol_ref[...] + (col0 + c0)
        ok = row_ok & (kcol >= 0) & (kcol < width)
        bias = inside_ref[...] + jnp.where(ok, 0.0, -jnp.inf)
        bias = jnp.concatenate([bias, bias], axis=0)
        for pair in range(channels // 128):
            lanes = slice(128 * pair, 128 * pair + 128)
            qp = qs[:, pl.ds(c0, QC), lanes].reshape(ROWS * QC, 128)
            zero = jnp.zeros_like(qp)
            q2 = jnp.concatenate([jnp.where(low, qp, zero), jnp.where(low, zero, qp)], axis=0)
            kp = kv[:, pl.ds(c0, KC), lanes].reshape(SPAN * KC, 128).astype(jnp.bfloat16)
            vp = kv[:, pl.ds(c0, KC), channels + 128 * pair:channels + 128 * pair + 128].reshape(SPAN * KC, 128).astype(jnp.bfloat16)
            s = lax.dot_general(q2, kp, (((1,), (1,)), ((), ())), preferred_element_type=jnp.float32) + bias
            p = jnp.exp(s - jnp.max(s, axis=-1, keepdims=True)).astype(jnp.bfloat16)
            o = jnp.dot(p, jnp.concatenate([vp, ones], axis=1), preferred_element_type=jnp.float32)
            half = ROWS * QC
            num = jnp.where(low, o[:half, :128], o[half:, :128])
            den = jnp.where(low, o[:half, 128:], o[half:, 128:])
            mix[:, pl.ds(c0, QC), lanes] = (num / den).astype(jnp.bfloat16).reshape(ROWS, QC, 128)
        return carry

    lax.fori_loop(0, breadth // QC, block, 0)
    out = jnp.dot(mix[...].reshape(ROWS * breadth, channels), wo_ref[...], preferred_element_type=jnp.float32)
    out_ref[...] = (tok[3:3 + ROWS].astype(jnp.float32).reshape(ROWS * breadth, channels) + out).astype(jnp.bfloat16)

def window_call(place, gain, wq, wk, wv, wo, parts):
    plan, srcs, edges, at = [], [], [], 0
    for array, edge, first, count in parts:
        plan.append((at, first, count))
        srcs.append(array)
        edges.append(edge)
        at += count
    breadth, channels = srcs[0].shape[1:]
    wide = breadth + 8
    n = np.arange(SPAN * KC)
    m = np.arange(ROWS * QC)
    rg = n[None] // KC - m[:, None] // QC
    cg = n[None] % KC - m[:, None] % QC
    inside = np.where((rg >= 0) & (rg <= 6) & (cg >= 0) & (cg <= 6), 0.0, -np.inf).astype(np.float32)
    keyrow = (n // KC - 3).astype(np.int32)[None]
    keycol = (n % KC - 3).astype(np.int32)[None]
    vm = pl.BlockSpec(memory_space=pltpu.VMEM)
    return pl.pallas_call(
        functools.partial(window_kernel, tuple(plan)),
        out_shape=jax.ShapeDtypeStruct((ROWS * breadth, channels), jnp.bfloat16),
        in_specs=[pl.BlockSpec(memory_space=pltpu.SMEM)] + [vm] * 8 + [pl.BlockSpec(memory_space=pl.ANY)] * (2 * len(srcs)),
        out_specs=vm,
        scratch_shapes=[
            pltpu.VMEM((SPAN, breadth, channels), jnp.bfloat16),
            pltpu.VMEM((SPAN, 8, channels), jnp.bfloat16),
            pltpu.VMEM((SPAN, wide, channels), jnp.float32),
            pltpu.VMEM((ROWS, breadth, channels), jnp.bfloat16),
            pltpu.VMEM((SPAN, wide, 2 * channels), jnp.float32),
            pltpu.VMEM((ROWS, breadth, channels), jnp.bfloat16),
            pltpu.SemaphoreType.DMA((2 * len(srcs),)),
        ],
        compiler_params=pltpu.CompilerParams(vmem_limit_bytes=48 << 20),
    )(place, jnp.asarray(inside), jnp.asarray(keyrow), jnp.asarray(keycol), gain.reshape(1, -1), wq, wk, wv, wo, *srcs, *edges)


TILE = 16

def gather_kernel(n_pieces, piece_rows, *refs):
    idx_ref, w_ref, qa_ref, ta_ref, sgain_ref, cgain_ref, wk_ref, wv_ref, wo_ref = refs[:9]
    pieces = refs[9:9 + n_pieces]
    joined_ref, normed_ref, stage, table, res, sems = refs[9 + n_pieces:]
    t = pl.program_id(0)
    tiles = pl.num_programs(0)
    breadth = tiles * TILE
    rows = TILE * TILE
    channels = res.shape[1]
    total = TILE * breadth

    @pl.when(t == 0)
    def _():
        slots = stage.shape[0]
        def copy(n):
            return pltpu.make_async_copy(pieces[n], stage.at[n % slots], sems.at[n % slots])
        for n in range(min(slots, n_pieces)):
            copy(n).start()
        for n in range(n_pieces):
            copy(n).wait()
            table[pl.ds(n * piece_rows, piece_rows), :] = stage[n % slots].astype(jnp.float32)
            if n + slots < n_pieces:
                copy(n + slots).start()

    def line(i, carry):
        base = i * breadth + t * TILE
        out0 = pl.multiple_of(i * TILE, TILE)
        for j in range(TILE):
            acc = None
            for k in range(4):
                at = k * total + base + j
                term = w_ref[at] * table[pl.ds(idx_ref[at], 1), :]
                acc = term if acc is None else acc + term
            res[pl.ds(out0 + j, 1), :] = acc
        return carry

    lax.fori_loop(0, TILE, line, 0)
    r = res[...].astype(jnp.bfloat16).astype(jnp.float32)
    nr = rms_rows(r, sgain_ref[...]).astype(jnp.bfloat16)
    kk = jnp.dot(nr, wk_ref[...], preferred_element_type=jnp.float32).astype(jnp.bfloat16)
    vv = jnp.dot(nr, wv_ref[...], preferred_element_type=jnp.float32).astype(jnp.bfloat16)
    qa = qa_ref[...].reshape(rows, channels)
    ones = jnp.ones((rows, 128), jnp.bfloat16)
    part = 128
    low = lax.broadcasted_iota(jnp.int32, (part, 128), 1) < 64
    mixes = []
    for pair in range(channels // 128):
        lanes = slice(128 * pair, 128 * pair + 128)
        kp, v2 = kk[:, lanes], jnp.concatenate([vv[:, lanes], ones], axis=1)
        halves = []
        for q0 in range(0, rows, part):
            qp = qa[q0:q0 + part, lanes]
            zero = jnp.zeros_like(qp)
            q2 = jnp.concatenate([jnp.where(low, qp, zero), jnp.where(low, zero, qp)], axis=0)
            s = lax.dot_general(q2, kp, (((1,), (1,)), ((), ())), preferred_element_type=jnp.float32)
            p = jnp.exp(s - jnp.max(s, axis=-1, keepdims=True)).astype(jnp.bfloat16)
            o = jnp.dot(p, v2, preferred_element_type=jnp.float32)
            num = jnp.where(low, o[:part, :128], o[part:, :128])
            den = jnp.where(low, o[:part, 128:], o[part:, 128:])
            halves.append((num / den).astype(jnp.bfloat16))
        mixes.append(jnp.concatenate(halves, axis=0))
    mix = jnp.concatenate(mixes, axis=1)
    out = jnp.dot(mix, wo_ref[...], preferred_element_type=jnp.float32)
    joined = (ta_ref[...].reshape(rows, channels).astype(jnp.float32) + out).astype(jnp.bfloat16)
    joined_ref[...] = joined.reshape(TILE, TILE, channels)
    normed_ref[...] = rms_rows(joined.astype(jnp.float32), cgain_ref[...]).astype(jnp.bfloat16).reshape(TILE, TILE, channels)

def gather_call(idx, weights, qa, ta, sgain, cgain, wk, wv, wo, pieces):
    height, breadth, channels = ta.shape
    piece_rows = pieces[0].shape[0]
    n = len(pieces)
    sm = pl.BlockSpec(memory_space=pltpu.SMEM)
    vm = pl.BlockSpec(memory_space=pltpu.VMEM)
    tile = pl.BlockSpec((TILE, TILE, channels), lambda t: (0, t, 0))
    shape = jax.ShapeDtypeStruct((height, breadth, channels), jnp.bfloat16)
    return pl.pallas_call(
        functools.partial(gather_kernel, n, piece_rows),
        grid=(breadth // TILE,),
        out_shape=(shape, shape),
        in_specs=[sm, sm, tile, tile] + [vm] * 5 + [pl.BlockSpec(memory_space=pl.ANY)] * n,
        out_specs=(tile, tile),
        scratch_shapes=[
            pltpu.VMEM((8, piece_rows, channels), jnp.bfloat16),
            pltpu.VMEM((n * piece_rows, channels), jnp.float32),
            pltpu.VMEM((TILE * TILE, channels), jnp.float32),
            pltpu.SemaphoreType.DMA((8,)),
        ],
        compiler_params=pltpu.CompilerParams(vmem_limit_bytes=48 << 20),
    )(idx, weights, qa, ta, sgain.reshape(1, -1), cgain.reshape(1, -1), wk, wv, wo, *pieces)


SIDE = 8

def gelu(x):
    return 0.5 * x * (1.0 + jnp.tanh(0.7978845608028654 * (x + 0.044715 * (x * x * x))))

def conv_rows(src, row, count, w_ref):
    span, channels = src.shape[1], src.shape[2]
    lhs = jnp.concatenate([src[row + a:row + a + count] if isinstance(row, int) else src[pl.ds(row + a, count)] for a in range(3)], axis=-1)
    y = jnp.dot(lhs.reshape(count * span, 3 * channels), w_ref[...], preferred_element_type=jnp.float32)
    y = y.reshape(count * span, 3 * channels)
    n = count * span
    return (pltpu.roll(y[:, :channels], 1, 0) + y[:, channels:2 * channels]
            + pltpu.roll(y[:, 2 * channels:], n - 1, 0)).reshape(count, span, channels)

def conv_kernel(place_ref, nc_ref, top_ref, bot_ref, side_ref, side_top_ref, side_bot_ref, joined_ref, w1_hbm, w2_hbm, out_ref,
                field, inner, w1, w2, sems):
    height, breadth, channels = nc_ref.shape
    span = field.shape[1]
    copies = []
    for n, (src, dst) in enumerate(((w1_hbm, w1), (w2_hbm, w2))):
        for a in range(3):
            for b in range(3):
                copies.append(pltpu.make_async_copy(
                    src.at[a, b], dst.at[pl.ds(a * channels, channels), pl.ds(b * channels, channels)],
                    sems.at[9 * n + 3 * a + b]))
    for c in copies:
        c.start()
    field[2:2 + height, SIDE:SIDE + breadth, :] = nc_ref[...]
    field[0:2, SIDE:SIDE + breadth, :] = top_ref[...]
    field[2 + height:4 + height, SIDE:SIDE + breadth, :] = bot_ref[...]
    row0, col0, total_h, total_w = place_ref[0], place_ref[1], place_ref[2], place_ref[3]
    for first_row, ref in ((0, side_top_ref), (2, side_ref), (2 + height, side_bot_ref)):
        edge = ref[...]
        zero = jnp.zeros_like(edge)
        rows = slice(first_row, first_row + edge.shape[0])
        field[rows, 0:SIDE, :] = jnp.where(col0 > 0, edge, zero)
        field[rows, SIDE + breadth:, :] = jnp.where(col0 + breadth < total_w, edge, zero)
    for c in copies[:9]:
        c.wait()
    col = lax.broadcasted_iota(jnp.int32, (1, span, 1), 1) + (col0 - SIDE)
    col_ok = (col >= 0) & (col < total_w)
    step1 = 3

    def first(n, carry):
        r = n * step1
        x = gelu(conv_rows(field, r, step1, w1))
        row = lax.broadcasted_iota(jnp.int32, (step1, 1, 1), 0) + (row0 - 1 + r)
        ok = (row >= 0) & (row < total_h) & col_ok
        inner[pl.ds(r, step1)] = jnp.where(ok, x, 0.0).astype(jnp.bfloat16)
        return carry

    lax.fori_loop(0, (height + 2) // step1, first, 0)
    for c in copies[9:]:
        c.wait()
    step2 = 4

    def second(n, carry):
        r = n * step2
        y = conv_rows(inner, r, step2, w2)[:, SIDE:SIDE + breadth, :]
        out_ref[pl.ds(r, step2)] = (joined_ref[pl.ds(r, step2)].astype(jnp.float32) + y).astype(jnp.bfloat16)
        return carry

    lax.fori_loop(0, height // step2, second, 0)

def conv_call(place, nc, top, bot, side, side_top, side_bot, joined, w1, w2):
    height, breadth, channels = nc.shape
    span = breadth + 2 * SIDE
    sm = pl.BlockSpec(memory_space=pltpu.SMEM)
    vm = pl.BlockSpec(memory_space=pltpu.VMEM)
    hb = pl.BlockSpec(memory_space=pl.ANY)
    return pl.pallas_call(
        conv_kernel,
        out_shape=jax.ShapeDtypeStruct(nc.shape, jnp.bfloat16),
        in_specs=[sm] + [vm] * 7 + [hb] * 2,
        out_specs=vm,
        scratch_shapes=[
            pltpu.VMEM((height + 4, span, channels), jnp.bfloat16),
            pltpu.VMEM((height + 2, span, channels), jnp.bfloat16),
            pltpu.VMEM((3 * channels, 3 * channels), jnp.bfloat16),
            pltpu.VMEM((3 * channels, 3 * channels), jnp.bfloat16),
            pltpu.SemaphoreType.DMA((18,)),
        ],
        compiler_params=pltpu.CompilerParams(vmem_limit_bytes=48 << 20),
    )(place, nc, top, bot, side, side_top, side_bot, joined, w1, w2)

def index_kernel(place_ref, slots_ref, weights_ref, tables_ref, index_ref, live_ref):
    swath, group, groups, cap, block = (place_ref[n] for n in range(5))
    lines = tables_ref.shape[1] - 1
    slots = slots_ref[...]
    peer, place = lax.div(slots, cap), lax.rem(slots, cap)
    step = lax.div(peer, groups) - swath
    other = jnp.where(lax.rem(peer, groups) == group, 0, 1)
    source = (step + 1) * 2 + other
    line, lane = source * lines + lax.div(place, 128), lax.rem(place, 128)
    cell = jnp.zeros_like(slots)
    count = jnp.zeros_like(slots)
    for s in range(6):
        count = jnp.where(source == s, jnp.broadcast_to(tables_ref[s, lines:lines + 1, :], slots.shape), count)
        for n in range(lines):
            row = jnp.broadcast_to(tables_ref[s, n:n + 1, :], slots.shape)
            picked = jnp.take_along_axis(row, lane, axis=1)
            cell = jnp.where(line == s * lines + n, picked, cell)
    toward = jnp.where(lax.rem(swath, 2) == 0, 1, -1)
    slot = jnp.where(step == 0, 0, jnp.where(step == toward, 1, 2))
    index_ref[...] = (slot * 2 + other) * block + cell
    live_ref[...] = jnp.where(place < count, weights_ref[...], 0.0)


def index_call(place, slots, weights, tables):
    sm = pl.BlockSpec(memory_space=pltpu.SMEM)
    vm = pl.BlockSpec(memory_space=pltpu.VMEM)
    return pl.pallas_call(
        index_kernel,
        out_shape=(jax.ShapeDtypeStruct(slots.shape, jnp.int32), jax.ShapeDtypeStruct(slots.shape, jnp.float32)),
        in_specs=[sm] + [vm] * 3,
        out_specs=(vm, vm),
    )(place, slots, weights, tables)


def rms_gain(values, gain_vector):
    return rms_rows(values.astype(jnp.float32), gain_vector).astype(jnp.bfloat16)


def body(
    tokens_b,
    tokens_a,
    pack_rows,
    pack_count,
    gather_slots,
    blend_weights,
    swath_gain,
    swath_query,
    swath_key,
    swath_value,
    swath_out,
    query_gain,
    source_gain,
    cross_query,
    cross_key,
    cross_value,
    cross_out,
    conv_gain,
    conv_first,
    conv_second,
):
    height, breadth, channels = tokens_b.shape
    swaths, groups = lax.axis_size("swath"), lax.axis_size("group")
    swath, group = lax.axis_index("swath"), lax.axis_index("group")
    assert groups == 2 and swaths % 2 == 0
    whole = [height * swaths, breadth * groups]
    down = [(i, i + 1) for i in range(swaths - 1)]
    up = [(j, i) for i, j in down]
    swap = [(0, 1), (1, 0)]
    pairs = [(i, i ^ 1) for i in range(swaths)]
    relay = [(i, j) for i in range(swaths) for j in [i + 2 if i % 2 == 0 else i - 2] if 0 <= j < swaths]
    cross = lambda moves: [(2 * i + g, 2 * j + 1 - g) for i, j in moves for g in (0, 1)]

    def inner_edge(field):
        start = (1 - group) * (breadth - SIDE)
        return lax.dynamic_slice_in_dim(field, start, SIDE, axis=1)

    def rims(field, width):
        edge = inner_edge(field)
        last, first = slice(height - width, height), slice(0, width)
        return (
            lax.ppermute(edge, "group", swap),
            lax.ppermute(field[last], "swath", down),
            lax.ppermute(field[first], "swath", up),
            lax.ppermute(edge[last], ("swath", "group"), cross(down)),
            lax.ppermute(edge[first], ("swath", "group"), cross(up)),
        )

    side, top, bottom, side_top, side_bottom = rims(tokens_b, 3)
    parts = {
        0: [(top, side_top, 0, 3), (tokens_b, side, 0, SPAN - 3)],
        height - ROWS: [(tokens_b, side, height - ROWS - 3, ROWS + 3), (bottom, side_bottom, 0, 3)],
    }
    chunks = {}
    order = [r for r in range(ROWS, height - ROWS, ROWS)] + [0, height - ROWS]
    for r in order:
        place = jnp.stack([swath * height + r, group * breadth, jnp.int32(whole[0]), jnp.int32(whole[1])]).astype(jnp.int32)
        chunks[r] = window_call(
            place, swath_gain, swath_query, swath_key, swath_value, swath_out,
            parts.get(r, [(tokens_b, side, r - 3, SPAN)]),
        )
    blocks = [{}, {}, {}]
    for r in order:
        mine = chunks[r]
        near = lax.ppermute(mine, "swath", pairs)
        far = lax.ppermute(near, "swath", relay)
        for at, rows in enumerate((mine, near, far)):
            blocks[at][r] = (rows, lax.ppermute(rows, "group", swap))
    pieces = [blocks[at][r][o] for at in range(3) for o in range(2) for r in sorted(order)]

    cap = pack_rows.shape[-1]
    lines = cap // 128
    tables = jnp.concatenate(
        [pack_rows.reshape(-1, lines, 128), jnp.broadcast_to(pack_count.reshape(-1, 1, 1), (pack_count.size, 1, 128))], axis=1
    ).reshape(swaths, groups, lines + 1, 128)
    pick = lambda step: lax.dynamic_index_in_dim(tables, jnp.clip(swath + step, 0, swaths - 1), 0, keepdims=False)
    held = jnp.stack([lax.ppermute(pick(1), "swath", down), pick(0), lax.ppermute(pick(-1), "swath", up)])
    here = lax.dynamic_index_in_dim(held, group, 1, keepdims=False)
    there = lax.ppermute(lax.dynamic_index_in_dim(held, 1 - group, 1, keepdims=False), "group", swap)
    tables = jnp.stack([here, there], axis=1).reshape(6, lines + 1, 128)
    place = jnp.stack([swath, group, jnp.int32(groups), jnp.int32(cap), jnp.int32(height * breadth)]).astype(jnp.int32)
    index, live = index_call(place, gather_slots.reshape(-1, 128), blend_weights.reshape(-1, 128), tables)

    normed_a = rms_gain(tokens_a, query_gain).reshape(-1, channels)
    query_a = jnp.dot(normed_a, cross_query, preferred_element_type=jnp.float32).astype(jnp.bfloat16)
    query_a = (query_a * jnp.bfloat16(0.125)).reshape(tokens_a.shape)
    joined, normed_c = gather_call(
        index.reshape(-1), live.reshape(-1), query_a, tokens_a, source_gain, conv_gain,
        cross_key, cross_value, cross_out, pieces,
    )
    side, top, bottom, side_top, side_bottom = rims(normed_c, 2)
    place = jnp.stack([swath * height, group * breadth, jnp.int32(whole[0]), jnp.int32(whole[1])]).astype(jnp.int32)
    return conv_call(place, normed_c, top, bottom, side, side_top, side_bottom, joined, conv_first, conv_second)


def solution(mesh):
    rows = P(("strip", "swath"), "group", None)
    maps = P(None, ("strip", "swath"), "group")
    placed = (rows, rows, P(("strip", "swath"), "group", None, None), rows, maps, maps) + (P(),) * 14
    return jax.shard_map(body, mesh=mesh, in_specs=placed, out_specs=rows, check_vma=False)
```

```python
import functools

import jax
import jax.numpy as jnp
import numpy as np
from jax import lax
from jax.experimental import pallas as pl
from jax.experimental.pallas import tpu as pltpu
from jax.sharding import PartitionSpec as P


EPSILON = 1e-06
ROWS = 4
SPAN = ROWS + 6
QC = 16
KC = 24
HD = 64

def rms_rows(x, gain):
    inv = lax.rsqrt(jnp.mean(x * x, axis=-1, keepdims=True) + EPSILON)
    return x * inv * gain

def attend_heads(q, k, v, bias):
    rows, lanes = q.shape
    heads = lanes // HD
    lane = lax.broadcasted_iota(jnp.int32, q.shape, 1) // HD
    zero = jnp.zeros_like(q)
    stacked = jnp.concatenate([jnp.where(lane == h, q, zero) for h in range(heads)], axis=0)
    s = lax.dot_general(stacked, k, (((1,), (1,)), ((), ())), preferred_element_type=jnp.float32)
    if bias is not None:
        s = s + jnp.concatenate([bias] * heads, axis=0)
    p = jnp.exp(s - jnp.max(s, axis=-1, keepdims=True))
    total = 1.0 / jnp.sum(p, axis=-1, keepdims=True)
    o = jnp.dot(p.astype(jnp.bfloat16), v, preferred_element_type=jnp.float32)
    mixed, scale = o[:rows], total[:rows]
    for h in range(1, heads):
        mixed = jnp.where(lane == h, o[h * rows:(h + 1) * rows], mixed)
        scale = jnp.where(lane == h, total[h * rows:(h + 1) * rows], scale)
    return mixed * scale

def window_kernel(first_row, plan, place_ref, gains_ref, wq_hbm, wk_hbm, wv_hbm, wo_hbm, *rest):
    n_src = len(plan)
    srcs, edges = rest[:n_src], rest[n_src:2 * n_src]
    out_ref, tok, side, normed, qs, kv, mix, wq, wk, wv, wo, sems, row_sems = rest[2 * n_src:]
    breadth, channels = tok.shape[1:]
    wide = normed.shape[1]
    copies, edge_copies = [], []
    for n, (dst0, src0, edge0, count) in enumerate(plan):
        edge_copies.append(pltpu.make_async_copy(edges[n].at[pl.ds(edge0, count)], side.at[pl.ds(dst0, count)], sems.at[4 + n]))
        for r in range(count):
            copies.append(pltpu.make_async_copy(srcs[n].at[src0 + r], tok.at[dst0 + r], row_sems.at[dst0 + r]))
    weights = [
        pltpu.make_async_copy(src, dst, sems.at[n])
        for n, (src, dst) in enumerate(((wq_hbm, wq), (wk_hbm, wk), (wv_hbm, wv), (wo_hbm, wo)))
    ]
    for c in edge_copies + copies + weights:
        c.start()
    gain = gains_ref[0:1, :]
    normed[:, breadth:, :] = jnp.zeros((SPAN, wide - breadth, channels), jnp.float32)
    n = lax.broadcasted_iota(jnp.int32, (1, SPAN * KC), 1)
    key_row = (n * 2731) >> 16
    key_col = n - key_row * KC
    m = lax.broadcasted_iota(jnp.int32, (ROWS * QC, 1), 0)
    row_gap, col_gap = key_row - (m >> 4), key_col - (m & 15)
    inside = (row_gap >= 0) & (row_gap <= 6) & (col_gap >= 0) & (col_gap <= 6)
    row0, col0, height, width = place_ref[0] + first_row, place_ref[1], place_ref[2], place_ref[3]
    row_at = key_row + (row0 - 3)
    inside = jnp.where(inside & (row_at >= 0) & (row_at < height), 0.0, -jnp.inf)
    for c in edge_copies:
        c.wait()
    for r in range(SPAN):
        copies[r].wait()
        x = rms_rows(tok[r].astype(jnp.float32), gain)
        normed[r, 3:3 + breadth, :] = x
        if 3 <= r < 3 + ROWS:
            qs[r - 3] = x.astype(jnp.bfloat16)
        x = rms_rows(side[r].astype(jnp.float32), gain)
        normed[r, 0:3, :] = x[5:8]
        normed[r, 3 + breadth:6 + breadth, :] = x[0:3]
    for c in weights:
        c.wait()
    q = jnp.dot(qs[...].reshape(ROWS * breadth, channels), wq[...], preferred_element_type=jnp.float32)
    qs[...] = (q.astype(jnp.bfloat16) * jnp.bfloat16(HD ** -0.5)).reshape(ROWS, breadth, channels)
    flat = normed[...].reshape(SPAN * wide, channels).astype(jnp.bfloat16)
    kv[:, :, :channels] = jnp.dot(flat, wk[...], preferred_element_type=jnp.float32).reshape(SPAN, wide, channels)
    kv[:, :, channels:] = jnp.dot(flat, wv[...], preferred_element_type=jnp.float32).reshape(SPAN, wide, channels)

    def block(cb, carry):
        c0 = pl.multiple_of(cb * QC, QC)
        col_at = key_col + (col0 + c0 - 3)
        bias = inside + jnp.where((col_at >= 0) & (col_at < width), 0.0, -jnp.inf)
        for l0, l1 in ((0, 256), (256, 384)):
            qp = qs[:, pl.ds(c0, QC), l0:l1].reshape(ROWS * QC, l1 - l0)
            kp = kv[:, pl.ds(c0, KC), l0:l1].reshape(SPAN * KC, l1 - l0).astype(jnp.bfloat16)
            vp = kv[:, pl.ds(c0, KC), channels + l0:channels + l1].reshape(SPAN * KC, l1 - l0).astype(jnp.bfloat16)
            mixed = attend_heads(qp, kp, vp, bias)
            mix[:, pl.ds(c0, QC), l0:l1] = mixed.astype(jnp.bfloat16).reshape(ROWS, QC, l1 - l0)
        return carry

    lax.fori_loop(0, breadth // QC, block, 0, unroll=True)
    out = jnp.dot(mix[...].reshape(ROWS * breadth, channels), wo[...], preferred_element_type=jnp.float32)
    out_ref[...] = (tok[3:3 + ROWS].astype(jnp.float32).reshape(ROWS * breadth, channels) + out).astype(jnp.bfloat16)

def window_call(place, gains, wq, wk, wv, wo, first_row, parts):
    plan, srcs, edges, at = [], [], [], 0
    for array, edge, first, edge_first, count in parts:
        plan.append((at, first, edge_first, count))
        srcs.append(array)
        edges.append(edge)
        at += count
    breadth, channels = srcs[0].shape[1:]
    wide = breadth + 8
    square = pltpu.VMEM((channels, channels), jnp.bfloat16)
    return pl.pallas_call(
        functools.partial(window_kernel, first_row, tuple(plan)),
        out_shape=jax.ShapeDtypeStruct((ROWS * breadth, channels), jnp.bfloat16),
        in_specs=[pl.BlockSpec(memory_space=pltpu.SMEM), pl.BlockSpec(memory_space=pltpu.VMEM)]
        + [pl.BlockSpec(memory_space=pltpu.HBM)] * 4 + [pl.BlockSpec(memory_space=pl.ANY)] * (2 * len(srcs)),
        out_specs=pl.BlockSpec(memory_space=pltpu.VMEM),
        scratch_shapes=[
            pltpu.VMEM((SPAN, breadth, channels), jnp.bfloat16),
            pltpu.VMEM((SPAN, 8, channels), jnp.bfloat16),
            pltpu.VMEM((SPAN, wide, channels), jnp.float32),
            pltpu.VMEM((ROWS, breadth, channels), jnp.bfloat16),
            pltpu.VMEM((SPAN, wide, 2 * channels), jnp.float32),
            pltpu.VMEM((ROWS, breadth, channels), jnp.bfloat16),
            square, square, square, square,
            pltpu.SemaphoreType.DMA((8,)),
            pltpu.SemaphoreType.DMA((SPAN,)),
        ],
        compiler_params=pltpu.CompilerParams(vmem_limit_bytes=60 << 20),
        cost_estimate=pl.CostEstimate(flops=8_000_000_000, transcendentals=0, bytes_accessed=4_000_000),
    )(place, gains, wq, wk, wv, wo, *srcs, *edges)


TILE = 16
PART = 64
RIM = 2
SIDE = 8
PIECE = 512

def gather_kernel(plan, n_arrays, piece_rows, *refs):
    place_ref, gains_ref, idx_hbm, w_hbm, qa_hbm, ta_hbm, wk_hbm, wv_hbm, wo_hbm = refs[:9]
    arrays = refs[9:9 + n_arrays]
    (joined_ref, normed_ref, top_ref, bottom_ref, edge_ref, table, res, keys, values, mix,
     idx_ref, w_ref, qa_ref, ta_ref, wk_ref, wv_ref, wo_ref, stage, sems, stage_sems) = refs[9 + n_arrays:]
    copies = [
        pltpu.make_async_copy(src, dst, sems.at[n])
        for n, (src, dst) in enumerate((
            (idx_hbm, idx_ref), (w_hbm, w_ref), (wk_hbm, wk_ref), (wv_hbm, wv_ref), (qa_hbm, qa_ref), (ta_hbm, ta_ref), (wo_hbm, wo_ref)))
    ]
    for c in copies:
        c.start()
    height, breadth, channels = ta_ref.shape
    tiles = breadth // TILE
    rows = TILE * TILE
    total = height * breadth
    lanes = channels // 128

    slots = stage.shape[0]

    def copy(n):
        which, first = plan[n]
        return pltpu.make_async_copy(arrays[which].at[pl.ds(first, piece_rows)], stage.at[n % slots], stage_sems.at[n % slots])

    for n in range(slots):
        copy(n).start()
    for n in range(len(plan)):
        copy(n).wait()
        x = stage[n % slots].astype(jnp.float32)
        for j in range(lanes):
            table[pl.ds(n * (piece_rows // 8), piece_rows // 8), j] = x[:, 128 * j:128 * j + 128].reshape(piece_rows // 8, 8, 128)
        if n + slots < len(plan):
            copy(n + slots).start()
    flat = table.reshape(table.shape[0] * lanes * 8, 128)
    out = res.reshape(res.shape[0] * lanes * 8, 128)

    for c in copies[:2]:
        c.wait()

    idx1, w1 = idx_ref.reshape(4 * total), w_ref.reshape(4 * total)

    def line(n, carry):
        row, col = lax.rem(n, TILE), lax.div(n, TILE) * TILE
        at0 = n * (TILE * lanes)
        for j in range(TILE):
            acc = None
            for k in range(4):
                at = k * total + row * breadth + col + j
                term = w1[at] * flat[pl.ds(idx1[at], lanes, stride=8), :]
                acc = term if acc is None else acc + term
            out[pl.ds(at0 + (j // 8) * (8 * lanes) + j % 8, lanes, stride=8), :] = acc
        return carry

    lax.fori_loop(0, tiles * TILE, line, 0)
    for c in copies[2:]:
        c.wait()

    def project(t, carry):
        r = jnp.concatenate([res[pl.ds(t * (rows // 8), rows // 8), j].reshape(rows, 128) for j in range(lanes)], axis=1)
        nr = rms_rows(r.astype(jnp.bfloat16).astype(jnp.float32), gains_ref[2:3, :]).astype(jnp.bfloat16)
        at = pl.ds(pl.multiple_of(t * rows, rows), rows)
        keys[at, :] = jnp.dot(nr, wk_ref[...], preferred_element_type=jnp.float32).astype(jnp.bfloat16)
        values[at, :] = jnp.dot(nr, wv_ref[...], preferred_element_type=jnp.float32).astype(jnp.bfloat16)
        return carry

    lax.fori_loop(0, tiles, project, 0, unroll=2)

    def attend(t, carry):
        at = pl.ds(pl.multiple_of(t * rows, rows), rows)
        qa = qa_ref[:, pl.ds(pl.multiple_of(t * TILE, TILE), TILE), :].reshape(rows, channels)
        for l0, l1 in ((0, 256), (256, 384)):
            kp, vp = keys[at, l0:l1], values[at, l0:l1]
            for q0 in range(0, rows, PART):
                mixed = attend_heads(qa[q0:q0 + PART, l0:l1], kp, vp, None)
                mix[pl.ds(pl.multiple_of(t * rows + q0, PART), PART), l0:l1] = mixed.astype(jnp.bfloat16)
        return carry

    lax.fori_loop(0, tiles, attend, 0, unroll=2)

    def finish(t, carry):
        at = pl.ds(pl.multiple_of(t * rows, rows), rows)
        cols = pl.ds(pl.multiple_of(t * TILE, TILE), TILE)
        o = jnp.dot(mix[at, :], wo_ref[...], preferred_element_type=jnp.float32)
        joined = (ta_ref[:, cols, :].reshape(rows, channels).astype(jnp.float32) + o).astype(jnp.bfloat16)
        joined_ref[:, cols, :] = joined.reshape(TILE, TILE, channels)
        normed_ref[:, cols, :] = rms_rows(joined.astype(jnp.float32), gains_ref[3:4, :]).astype(jnp.bfloat16).reshape(TILE, TILE, channels)
        return carry

    lax.fori_loop(0, tiles, finish, 0, unroll=2)
    top_ref[...] = normed_ref[0:RIM]
    bottom_ref[...] = normed_ref[height - RIM:height]
    first_group = place_ref[1] == 0
    edge_ref[...] = jnp.where(first_group, normed_ref[:, breadth - SIDE:, :], normed_ref[:, 0:SIDE, :])

def gather_call(idx, weights, place, qa, ta, gains, wk, wv, wo, pieces):
    height, breadth, channels = ta.shape
    arrays, plan = [], []
    for rows, first in pieces:
        which = [n for n, array in enumerate(arrays) if array is rows]
        plan.append((which[0] if which else len(arrays), first))
        arrays += [] if which else [rows]
    piece_rows = PIECE
    n = len(pieces)
    total = height * breadth
    lanes = channels // 128
    assert height == TILE and channels == 384
    sm = pl.BlockSpec(memory_space=pltpu.SMEM)
    anywhere = pl.BlockSpec(memory_space=pl.ANY)
    square = pltpu.VMEM((channels, channels), jnp.bfloat16)
    vm = pl.BlockSpec(memory_space=pltpu.VMEM)
    shape = jax.ShapeDtypeStruct((height, breadth, channels), jnp.bfloat16)
    rim = jax.ShapeDtypeStruct((RIM, breadth, channels), jnp.bfloat16)
    return pl.pallas_call(
        functools.partial(gather_kernel, tuple(plan), len(arrays), piece_rows),
        out_shape=(shape, shape, rim, rim, jax.ShapeDtypeStruct((height, SIDE, channels), jnp.bfloat16)),
        in_specs=[sm, vm] + [anywhere] * 3 + [pl.BlockSpec(memory_space=pltpu.HBM)] * 4 + [anywhere] * len(arrays),
        out_specs=(vm,) * 5,
        scratch_shapes=[
            pltpu.VMEM((n * piece_rows // 8, lanes, 8, 128), jnp.float32),
            pltpu.VMEM((total // 8, lanes, 8, 128), jnp.float32),
            pltpu.VMEM((total, channels), jnp.bfloat16),
            pltpu.VMEM((total, channels), jnp.bfloat16),
            pltpu.VMEM((total, channels), jnp.bfloat16),
            pltpu.SMEM(idx.shape, jnp.int32),
            pltpu.SMEM(idx.shape, jnp.float32),
            pltpu.VMEM(ta.shape, jnp.bfloat16),
            pltpu.VMEM(ta.shape, jnp.bfloat16),
            square, square, square,
            pltpu.VMEM((8, piece_rows, channels), jnp.bfloat16),
            pltpu.SemaphoreType.DMA((7,)),
            pltpu.SemaphoreType.DMA((8,)),
        ],
        compiler_params=pltpu.CompilerParams(vmem_limit_bytes=60 << 20),
        cost_estimate=pl.CostEstimate(flops=30_000_000_000, transcendentals=0, bytes_accessed=10_000_000),
    )(place, gains, idx, weights, qa, ta, wk, wv, wo, *arrays)


def gelu(x):
    return 0.5 * x * (1.0 + jnp.tanh(0.7978845608028654 * (x + 0.044715 * (x * x * x))))

def tap_copies(src, dst, sems):
    channels = src.shape[-1]
    return [
        pltpu.make_async_copy(
            src.at[a, b], dst.at[pl.ds(a * channels, channels), pl.ds(b * channels, channels)], sems.at[3 * a + b])
        for a in range(3) for b in range(3)
    ]

def conv_rows(src, row, count, w_ref):
    span, channels = src.shape[1], src.shape[2]
    lhs = jnp.concatenate([src[pl.ds(row + a, count)] for a in range(3)], axis=-1)
    n = count * span
    y = jnp.dot(lhs.reshape(n, 3 * channels), w_ref[...], preferred_element_type=jnp.float32)
    return (pltpu.roll(y[:, :channels], 1, 0) + y[:, channels:2 * channels]
            + pltpu.roll(y[:, 2 * channels:], n - 1, 0)).reshape(count, span, channels)

def place_sides(field, rows, edge, place_ref, breadth):
    zero = jnp.zeros_like(edge)
    field[rows, 0:SIDE, :] = jnp.where(place_ref[1] > 0, edge, zero)
    field[rows, SIDE + breadth:, :] = jnp.where(place_ref[1] + breadth < place_ref[3], edge, zero)

def columns_inside(place_ref, span):
    col = lax.broadcasted_iota(jnp.int32, (1, span, 1), 1) + (place_ref[1] - SIDE)
    return (col >= 0) & (col < place_ref[3])

def first_kernel(place_ref, nc_ref, side_ref, w_hbm, inner_ref, field, w, sems):
    height, breadth, channels = nc_ref.shape
    span = field.shape[1]
    copies = tap_copies(w_hbm, w, sems)
    for c in copies:
        c.start()
    field[:, SIDE:SIDE + breadth, :] = nc_ref[...]
    place_sides(field, slice(0, height), side_ref[...], place_ref, breadth)
    ok = columns_inside(place_ref, span)
    for c in copies:
        c.wait()
    step = 2

    def rows(n, carry):
        x = gelu(conv_rows(field, n * step, step, w))
        inner_ref[pl.ds(n * step, step)] = jnp.where(ok, x, 0.0).astype(jnp.bfloat16)
        return carry

    lax.fori_loop(0, (height - 2) // step, rows, 0)

def second_kernel(inner_ref, joined_ref, w_hbm, out_ref, w, sems):
    height, breadth, channels = joined_ref.shape
    copies = tap_copies(w_hbm, w, sems)
    for c in copies:
        c.start()
    for c in copies:
        c.wait()
    step = 2

    def rows(n, carry):
        y = conv_rows(inner_ref, n * step, step, w)[:, SIDE:SIDE + breadth, :]
        at = pl.ds(n * step + RIM, step)
        out_ref[at] = (joined_ref[at].astype(jnp.float32) + y).astype(jnp.bfloat16)
        return carry

    lax.fori_loop(0, (height - 2 * RIM) // step, rows, 0)

def rim_kernel(place_ref, nc_ref, side_ref, top_ref, bottom_ref, side_rim_ref, inner_ref, joined_ref,
               w1_hbm, w2_hbm, merged_hbm, out_hbm, field, inner, done, w1, w2, sems1, sems2, out_sems):
    height, breadth, channels = joined_ref.shape
    span = field.shape[1]
    copies1, copies2 = tap_copies(w1_hbm, w1, sems1), tap_copies(w2_hbm, w2, sems2)
    for c in copies1 + copies2:
        c.start()
    ok = columns_inside(place_ref, span)
    for c in copies1:
        c.wait()
    for end in range(2):
        own = 0 if end == 0 else height - RIM
        own_at, far_at = (RIM, 0) if end == 0 else (0, RIM)
        far = top_ref if end == 0 else bottom_ref
        field[own_at:own_at + RIM, SIDE:SIDE + breadth, :] = nc_ref[own:own + RIM]
        place_sides(field, slice(own_at, own_at + RIM), side_ref[own:own + RIM], place_ref, breadth)
        field[far_at:far_at + RIM, SIDE:SIDE + breadth, :] = far[...]
        place_sides(field, slice(far_at, far_at + RIM), side_rim_ref[end * RIM:end * RIM + RIM], place_ref, breadth)
        x = gelu(conv_rows(field, 0, RIM, w1))
        row = lax.broadcasted_iota(jnp.int32, (RIM, 1, 1), 0) + (place_ref[0] + (-1 if end == 0 else height - 1))
        x = jnp.where((row >= 0) & (row < place_ref[2]) & ok, x, 0.0).astype(jnp.bfloat16)
        if end == 0:
            inner[0:RIM] = x
            inner[RIM:2 * RIM] = inner_ref[0:RIM]
        else:
            inner[0:RIM] = inner_ref[height - 2 - RIM:height - 2]
            inner[RIM:2 * RIM] = x
        if end == 0:
            for c in copies2:
                c.wait()
        y = conv_rows(inner, 0, RIM, w2)[:, SIDE:SIDE + breadth, :]
        done[end] = (joined_ref[own:own + RIM].astype(jnp.float32) + y).astype(jnp.bfloat16)
        pltpu.make_async_copy(done.at[end], out_hbm.at[pl.ds(own, RIM)], out_sems.at[end]).start()
    for end in range(2):
        own = 0 if end == 0 else height - RIM
        pltpu.make_async_copy(done.at[end], out_hbm.at[pl.ds(own, RIM)], out_sems.at[end]).wait()

SM = pl.BlockSpec(memory_space=pltpu.SMEM)
VM = pl.BlockSpec(memory_space=pltpu.VMEM)
HB = pl.BlockSpec(memory_space=pl.ANY)

def first_call(place, nc, side, w1):
    height, breadth, channels = nc.shape
    span = breadth + 2 * SIDE
    return pl.pallas_call(
        first_kernel,
        out_shape=jax.ShapeDtypeStruct((height - 2, span, channels), jnp.bfloat16),
        in_specs=[SM, VM, VM, HB],
        out_specs=VM,
        scratch_shapes=[
            pltpu.VMEM((height, span, channels), jnp.bfloat16),
            pltpu.VMEM((3 * channels, 3 * channels), jnp.bfloat16),
            pltpu.SemaphoreType.DMA((9,)),
        ],
        compiler_params=pltpu.CompilerParams(vmem_limit_bytes=40 << 20),
        cost_estimate=pl.CostEstimate(flops=10_000_000_000, transcendentals=0, bytes_accessed=4_000_000),
    )(place, nc, side, w1)

def second_call(inner, joined, w2):
    channels = joined.shape[-1]
    return pl.pallas_call(
        second_kernel,
        out_shape=jax.ShapeDtypeStruct(joined.shape, jnp.bfloat16),
        in_specs=[VM, VM, HB],
        out_specs=VM,
        scratch_shapes=[pltpu.VMEM((3 * channels, 3 * channels), jnp.bfloat16), pltpu.SemaphoreType.DMA((9,))],
        compiler_params=pltpu.CompilerParams(vmem_limit_bytes=40 << 20),
        cost_estimate=pl.CostEstimate(flops=8_000_000_000, transcendentals=0, bytes_accessed=4_000_000),
    )(inner, joined, w2)

def rim_call(place, nc, side, top, bottom, side_rim, inner, joined, w1, w2, merged):
    height, breadth, channels = nc.shape
    span = breadth + 2 * SIDE
    return pl.pallas_call(
        rim_kernel,
        out_shape=jax.ShapeDtypeStruct(joined.shape, jnp.bfloat16),
        in_specs=[SM] + [VM] * 7 + [HB] * 3,
        out_specs=HB,
        input_output_aliases={10: 0},
        scratch_shapes=[
            pltpu.VMEM((2 * RIM, span, channels), jnp.bfloat16),
            pltpu.VMEM((2 * RIM, span, channels), jnp.bfloat16),
            pltpu.VMEM((2, RIM, breadth, channels), jnp.bfloat16),
            pltpu.VMEM((3 * channels, 3 * channels), jnp.bfloat16),
            pltpu.VMEM((3 * channels, 3 * channels), jnp.bfloat16),
            pltpu.SemaphoreType.DMA((9,)),
            pltpu.SemaphoreType.DMA((9,)),
            pltpu.SemaphoreType.DMA((2,)),
        ],
        compiler_params=pltpu.CompilerParams(vmem_limit_bytes=40 << 20),
        cost_estimate=pl.CostEstimate(flops=5_000_000_000, transcendentals=0, bytes_accessed=4_000_000),
    )(place, nc, side, top, bottom, side_rim, inner, joined, w1, w2, merged)

def pack_kernel(place_ref, rows_ref, count_ref, keep_ref, give_ref):
    swath, group, groups = place_ref[4], place_ref[5], place_ref[6]
    peers, cap = rows_ref.shape
    lines = cap // 128
    for step in range(3):
        near = jnp.clip(swath + step - 1, 0, peers // groups - 1) * groups
        for ref, at in ((keep_ref, near + group), (give_ref, near + 1 - group)):
            row = rows_ref[pl.ds(at, 1), :]
            for n in range(lines):
                ref[step, n:n + 1, :] = row[:, 128 * n:128 * n + 128]
            ref[step, lines:lines + 1, :] = jnp.full((1, 128), count_ref[0, at], jnp.int32)


def pack_call(place, rows, count):
    sm = pl.BlockSpec(memory_space=pltpu.SMEM)
    vm = pl.BlockSpec(memory_space=pltpu.VMEM)
    shape = jax.ShapeDtypeStruct((3, rows.shape[1] // 128 + 1, 128), jnp.int32)
    return pl.pallas_call(
        pack_kernel, out_shape=(shape, shape), in_specs=[sm, vm, sm], out_specs=(vm, vm),
        cost_estimate=pl.CostEstimate(flops=1_000_000, transcendentals=0, bytes_accessed=100_000),
    )(place, rows, count)


def index_kernel(place_ref, slots_ref, weights_ref, upper_ref, keep_ref, taken_ref, lower_ref, index_ref, live_ref):
    swath, group, groups, cap, block = (place_ref[n] for n in range(4, 9))
    lines = keep_ref.shape[1] - 1
    blocks = ((upper_ref, 0), (upper_ref, 1), (keep_ref, 1), (taken_ref, 1), (lower_ref, 0), (lower_ref, 1))
    slots = slots_ref[...]
    peer, place = lax.div(slots, cap), lax.rem(slots, cap)
    step = lax.div(peer, groups) - swath
    other = jnp.where(lax.rem(peer, groups) == group, 0, 1)
    source = (step + 1) * 2 + other
    line, lane = source * lines + lax.div(place, 128), lax.rem(place, 128)
    cell = jnp.zeros_like(slots)
    count = jnp.zeros_like(slots)
    for s, (ref, at) in enumerate(blocks):
        count = jnp.where(source == s, jnp.broadcast_to(ref[at, lines:lines + 1, :], slots.shape), count)
        for n in range(lines):
            row = jnp.broadcast_to(ref[at, n:n + 1, :], slots.shape)
            picked = jnp.take_along_axis(row, lane, axis=1)
            cell = jnp.where(line == s * lines + n, picked, cell)
    toward = jnp.where(lax.rem(swath, 2) == 0, 1, -1)
    slot = jnp.where(step == 0, 0, jnp.where(step == toward, 1, 2))
    row = (slot * 2 + other) * block + cell
    index_ref[...] = lax.div(row, 8) * (8 * 3) + lax.rem(row, 8)
    live_ref[...] = jnp.where(place < count, weights_ref[...], 0.0)


def index_call(place, slots, weights, tables):
    sm = pl.BlockSpec(memory_space=pltpu.SMEM)
    vm = pl.BlockSpec(memory_space=pltpu.VMEM)
    return pl.pallas_call(
        index_kernel,
        out_shape=(jax.ShapeDtypeStruct(slots.shape, jnp.int32), jax.ShapeDtypeStruct(slots.shape, jnp.float32)),
        in_specs=[sm] + [vm] * 6,
        out_specs=(vm, vm),
        cost_estimate=pl.CostEstimate(flops=1_000_000, transcendentals=0, bytes_accessed=100_000),
    )(place, slots, weights, *tables)


def query_kernel(tokens_ref, gains_ref, w_ref, out_ref):
    height, breadth, channels = tokens_ref.shape
    for r in range(0, height, 4):
        x = rms_rows(tokens_ref[r:r + 4].reshape(4 * breadth, channels).astype(jnp.float32), gains_ref[1:2, :]).astype(jnp.bfloat16)
        q = jnp.dot(x, w_ref[...], preferred_element_type=jnp.float32).astype(jnp.bfloat16)
        out_ref[r:r + 4] = (q * jnp.bfloat16(HD ** -0.5)).reshape(4, breadth, channels)


def query_call(tokens, gains, w):
    return pl.pallas_call(
        query_kernel,
        out_shape=jax.ShapeDtypeStruct(tokens.shape, jnp.bfloat16),
        in_specs=[VM] * 3,
        out_specs=VM,
        compiler_params=pltpu.CompilerParams(vmem_limit_bytes=32 << 20),
        cost_estimate=pl.CostEstimate(flops=1_000_000, transcendentals=0, bytes_accessed=4_000_000),
    )(tokens, gains, w)


def body(
    tokens_b,
    tokens_a,
    pack_rows,
    pack_count,
    gather_slots,
    blend_weights,
    swath_gain,
    swath_query,
    swath_key,
    swath_value,
    swath_out,
    query_gain,
    source_gain,
    cross_query,
    cross_key,
    cross_value,
    cross_out,
    conv_gain,
    conv_first,
    conv_second,
):
    height, breadth, channels = tokens_b.shape
    swaths, groups = lax.axis_size("swath"), lax.axis_size("group")
    swath, group = lax.axis_index("swath"), lax.axis_index("group")
    assert groups == 2 and swaths % 2 == 0
    whole = [height * swaths, breadth * groups]
    down = [(i, i + 1) for i in range(swaths - 1)]
    up = [(j, i) for i, j in down]
    swap = [(0, 1), (1, 0)]
    pairs = [(i, i ^ 1) for i in range(swaths)]
    relay = [(i, j) for i in range(swaths) for j in [i + 2 if i % 2 == 0 else i - 2] if 0 <= j < swaths]

    def inner_edge(field):
        start = (1 - group) * (breadth - SIDE)
        return lax.dynamic_slice_in_dim(field, start, SIDE, axis=1)

    def after(values, *results):
        return lax.optimization_barrier((values, *results))[0]

    cap = pack_rows.shape[-1]
    place = jnp.stack([
        swath * height, group * breadth, jnp.int32(whole[0]), jnp.int32(whole[1]),
        swath, group, jnp.int32(groups), jnp.int32(cap), jnp.int32(height * breadth),
    ]).astype(jnp.int32)
    row = lax.broadcasted_iota(jnp.int32, (8, channels), 0)
    gains = sum(jnp.where(row == n, gain[None, :], 0.0) for n, gain in enumerate((swath_gain, query_gain, source_gain, conv_gain)))

    margin = 3
    side = lax.ppermute(inner_edge(tokens_b), "group", swap)
    top = lax.ppermute(tokens_b[height - margin:], "swath", down)
    bottom = lax.ppermute(tokens_b[:margin], "swath", up)
    chunks = {}

    def window(r, parts, *results):
        chunks[r] = window_call(
            after(place, *results) if results else place, gains, swath_query, swath_key, swath_value, swath_out, r, parts
        )
        return chunks[r]

    def near(rows):
        return lax.ppermute(rows, "swath", pairs)

    def far(rows):
        return lax.ppermute(rows, "swath", relay)

    r0, r1, r2, r3 = range(0, height, ROWS)
    window(r1, [(tokens_b, side, r1 - margin, r1 - margin, SPAN)])
    near1 = near(chunks[r1])
    rims = after(jnp.concatenate([top, bottom], axis=0), chunks[r1])
    rims = lax.ppermute(inner_edge(rims), "group", swap)
    window(r2, [(tokens_b, side, r2 - margin, r2 - margin, SPAN)])
    near2 = near(chunks[r2])
    far1 = far(near1)
    window(r0, [(top, rims, 0, 0, margin), (tokens_b, side, 0, 0, SPAN - margin)], chunks[r2], near1)
    near0 = near(chunks[r0])
    window(r3, [(tokens_b, side, r3 - margin, r3 - margin, SPAN - margin), (bottom, rims, 0, margin, margin)], chunks[r0], far1)
    near3 = near(chunks[r3])

    pack_rows, pack_count = after((pack_rows, pack_count), chunks[r3])
    keep, give = pack_call(place, pack_rows.reshape(-1, cap), pack_count.reshape(1, -1))
    taken = lax.ppermute(give, "group", swap)
    upper = lax.ppermute(jnp.concatenate([keep[2:], taken[2:]], axis=0), "swath", down)
    lower = lax.ppermute(jnp.concatenate([keep[:1], taken[:1]], axis=0), "swath", up)
    tokens_a = after(tokens_a, chunks[r3])
    index, live = index_call(
        place, gather_slots.reshape(-1, 128), blend_weights.reshape(-1, 128), (upper, keep, taken, lower)
    )
    query_a = query_call(tokens_a, gains, cross_query)

    far2 = far(near2)
    far0 = far(near0)
    far3 = far(near3)
    swapped = lambda rows: lax.ppermute(rows, "group", swap)
    other = [[swapped(rows) for rows in (group_rows)] for group_rows in ((chunks[r0], chunks[r1], chunks[r2], chunks[r3]), (near0, near1, near2, near3), (far0, far1, far2))]
    far3, index, live, query_a = lax.optimization_barrier((far3, index, live, query_a))
    other[2].append(swapped(far3))
    pieces = [chunks[r] for r in (r0, r1, r2, r3)] + other[0] + [near0, near1, near2, near3] + other[1] + [far0, far1, far2, far3] + other[2]
    pieces = [(rows, 0) for rows in pieces]
    joined, normed_c, first_rows, last_rows, edge = gather_call(
        index, live, place, query_a, tokens_a, gains,
        cross_key, cross_value, cross_out, pieces,
    )

    side = lax.ppermute(edge, "group", swap)
    top = lax.ppermute(last_rows, "swath", down)
    bottom = lax.ppermute(first_rows, "swath", up)
    inner = first_call(place, normed_c, side, conv_first)
    rims = after(jnp.concatenate([top, bottom], axis=0), inner)
    rims = lax.ppermute(inner_edge(rims), "group", swap)
    merged = second_call(inner, joined, conv_second)
    return rim_call(place, normed_c, side, top, bottom, rims, inner, joined, conv_first, conv_second, merged)


def solution(mesh):
    rows = P(("strip", "swath"), "group", None)
    maps = P(None, ("strip", "swath"), "group")
    placed = (rows, rows, P(("strip", "swath"), "group", None, None), rows, maps, maps) + (P(),) * 14
    return jax.shard_map(body, mesh=mesh, in_specs=placed, out_specs=rows, check_vma=False)
```

```python
import functools

import jax
import jax.numpy as jnp
import numpy as np
from jax import lax
from jax.experimental import pallas as pl
from jax.experimental.pallas import tpu as pltpu
from jax.sharding import PartitionSpec as P


EPSILON = 1e-06
ROWS = 4
SPAN = ROWS + 6
QC = 16
KC = 24
HD = 64

def rms_rows(x, gain):
    inv = lax.rsqrt(jnp.mean(x * x, axis=-1, keepdims=True) + EPSILON)
    return x * inv * gain

def attend_heads(q, k, v, bias):
    rows, lanes = q.shape
    heads = lanes // HD
    lane = lax.broadcasted_iota(jnp.int32, q.shape, 1) // HD
    zero = jnp.zeros_like(q)
    stacked = jnp.concatenate([jnp.where(lane == h, q, zero) for h in range(heads)], axis=0)
    s = lax.dot_general(stacked, k, (((1,), (1,)), ((), ())), preferred_element_type=jnp.float32)
    if bias is not None:
        s = s + jnp.concatenate([bias] * heads, axis=0)
    p = jnp.exp(s - jnp.max(s, axis=-1, keepdims=True))
    total = 1.0 / jnp.sum(p, axis=-1, keepdims=True)
    o = jnp.dot(p.astype(jnp.bfloat16), v, preferred_element_type=jnp.float32)
    mixed, scale = o[:rows], total[:rows]
    for h in range(1, heads):
        mixed = jnp.where(lane == h, o[h * rows:(h + 1) * rows], mixed)
        scale = jnp.where(lane == h, total[h * rows:(h + 1) * rows], scale)
    return mixed * scale

def window_kernel(spans, plan, place_ref, gains_ref, wq_hbm, wk_hbm, wv_hbm, wo_hbm, *rest):
    n_src = len(plan)
    srcs, edges = rest[:n_src], rest[n_src:2 * n_src]
    out_ref, tok, side, normed, qs, kv, mix, wq, wk, wv, wo, sems = rest[2 * n_src:]
    key_rows, breadth, channels = tok.shape
    wide = normed.shape[1]
    rows = ROWS * len(spans)
    copies = []
    for n, (dst0, src0, edge0, count) in enumerate(plan):
        copies.append(pltpu.make_async_copy(edges[n].at[pl.ds(edge0, count)], side.at[pl.ds(dst0, count)], sems.at[4 + 2 * n]))
        copies.append(pltpu.make_async_copy(srcs[n].at[pl.ds(src0, count)], tok.at[pl.ds(dst0, count)], sems.at[5 + 2 * n]))
    weights = [
        pltpu.make_async_copy(src, dst, sems.at[n])
        for n, (src, dst) in enumerate(((wq_hbm, wq), (wk_hbm, wk), (wv_hbm, wv), (wo_hbm, wo)))
    ]
    for c in copies + weights:
        c.start()
    gain = gains_ref[0:1, :]
    normed[:, breadth:, :] = jnp.zeros((key_rows, wide - breadth, channels), jnp.float32)
    n = lax.broadcasted_iota(jnp.int32, (1, SPAN * KC), 1)
    key_row = (n * 2731) >> 16
    key_col = n - key_row * KC
    m = lax.broadcasted_iota(jnp.int32, (ROWS * QC, 1), 0)
    row_gap, col_gap = key_row - (m >> 4), key_col - (m & 15)
    near = (row_gap >= 0) & (row_gap <= 6) & (col_gap >= 0) & (col_gap <= 6)
    row0, col0, height, width = place_ref[0], place_ref[1], place_ref[2], place_ref[3]
    for c in copies:
        c.wait()
    for r in range(key_rows):
        x = rms_rows(tok[r].astype(jnp.float32), gain)
        normed[r, 3:3 + breadth, :] = x
        for n_span, (_, key0) in enumerate(spans):
            if key0 + 3 <= r < key0 + 3 + ROWS:
                qs[n_span * ROWS + r - key0 - 3] = x.astype(jnp.bfloat16)
        x = rms_rows(side[r].astype(jnp.float32), gain)
        normed[r, 0:3, :] = x[5:8]
        normed[r, 3 + breadth:6 + breadth, :] = x[0:3]
    for c in weights:
        c.wait()
    q = jnp.dot(qs[...].reshape(rows * breadth, channels), wq[...], preferred_element_type=jnp.float32)
    qs[...] = (q.astype(jnp.bfloat16) * jnp.bfloat16(HD ** -0.5)).reshape(rows, breadth, channels)
    flat = normed[...].reshape(key_rows * wide, channels).astype(jnp.bfloat16)
    kv[:, :, :channels] = jnp.dot(flat, wk[...], preferred_element_type=jnp.float32).reshape(key_rows, wide, channels)
    kv[:, :, channels:] = jnp.dot(flat, wv[...], preferred_element_type=jnp.float32).reshape(key_rows, wide, channels)

    for n_span, (first_row, key0) in enumerate(spans):
        row_at = key_row + (row0 + first_row - 3)
        inside = jnp.where(near & (row_at >= 0) & (row_at < height), 0.0, -jnp.inf)
        own, keys = slice(n_span * ROWS, n_span * ROWS + ROWS), slice(key0, key0 + SPAN)

        def block(cb, carry):
            c0 = pl.multiple_of(cb * QC, QC)
            col_at = key_col + (col0 + c0 - 3)
            bias = inside + jnp.where((col_at >= 0) & (col_at < width), 0.0, -jnp.inf)
            for l0, l1 in ((0, 256), (256, 384)):
                qp = qs[own, pl.ds(c0, QC), l0:l1].reshape(ROWS * QC, l1 - l0)
                kp = kv[keys, pl.ds(c0, KC), l0:l1].reshape(SPAN * KC, l1 - l0).astype(jnp.bfloat16)
                vp = kv[keys, pl.ds(c0, KC), channels + l0:channels + l1].reshape(SPAN * KC, l1 - l0).astype(jnp.bfloat16)
                mixed = attend_heads(qp, kp, vp, bias)
                mix[own, pl.ds(c0, QC), l0:l1] = mixed.astype(jnp.bfloat16).reshape(ROWS, QC, l1 - l0)
            return carry

        lax.fori_loop(0, breadth // QC, block, 0, unroll=4)
    out = jnp.dot(mix[...].reshape(rows * breadth, channels), wo[...], preferred_element_type=jnp.float32)
    base = jnp.concatenate([tok[key0 + 3:key0 + 3 + ROWS] for _, key0 in spans], axis=0)
    out_ref[...] = (base.astype(jnp.float32).reshape(rows * breadth, channels) + out).astype(jnp.bfloat16)

def window_call(place, gains, wq, wk, wv, wo, spans, parts):
    plan, srcs, edges, at = [], [], [], 0
    for array, edge, first, edge_first, count in parts:
        plan.append((at, first, edge_first, count))
        srcs.append(array)
        edges.append(edge)
        at += count
    breadth, channels = srcs[0].shape[1:]
    wide = breadth + 8
    rows = ROWS * len(spans)
    square = pltpu.VMEM((channels, channels), jnp.bfloat16)
    return pl.pallas_call(
        functools.partial(window_kernel, tuple(spans), tuple(plan)),
        out_shape=jax.ShapeDtypeStruct((rows * breadth, channels), jnp.bfloat16),
        in_specs=[pl.BlockSpec(memory_space=pltpu.SMEM), pl.BlockSpec(memory_space=pltpu.VMEM)]
        + [pl.BlockSpec(memory_space=pltpu.HBM)] * 4 + [pl.BlockSpec(memory_space=pl.ANY)] * (2 * len(srcs)),
        out_specs=pl.BlockSpec(memory_space=pltpu.VMEM),
        scratch_shapes=[
            pltpu.VMEM((at, breadth, channels), jnp.bfloat16),
            pltpu.VMEM((at, 8, channels), jnp.bfloat16),
            pltpu.VMEM((at, wide, channels), jnp.float32),
            pltpu.VMEM((rows, breadth, channels), jnp.bfloat16),
            pltpu.VMEM((at, wide, 2 * channels), jnp.float32),
            pltpu.VMEM((rows, breadth, channels), jnp.bfloat16),
            square, square, square, square,
            pltpu.SemaphoreType.DMA((4 + 2 * len(srcs),)),
        ],
        compiler_params=pltpu.CompilerParams(vmem_limit_bytes=60 << 20),
        cost_estimate=pl.CostEstimate(flops=14_000_000_000, transcendentals=0, bytes_accessed=4_000_000),
    )(place, gains, wq, wk, wv, wo, *srcs, *edges)


TILE = 16
PART = 64
RIM = 2
SIDE = 8
PIECE = 512

def gather_kernel(plan, n_arrays, piece_rows, *refs):
    place_ref, gains_ref, idx_hbm, w_hbm, qa_hbm, ta_hbm, wk_hbm, wv_hbm, wo_hbm = refs[:9]
    arrays = refs[9:9 + n_arrays]
    (joined_ref, normed_ref, top_ref, bottom_ref, edge_ref, table, res, keys, values, mix,
     idx_ref, w_ref, qa_ref, ta_ref, wk_ref, wv_ref, wo_ref, stage, sems, stage_sems) = refs[9 + n_arrays:]
    copies = [
        pltpu.make_async_copy(src, dst, sems.at[n])
        for n, (src, dst) in enumerate((
            (idx_hbm, idx_ref), (w_hbm, w_ref), (wk_hbm, wk_ref), (wv_hbm, wv_ref), (qa_hbm, qa_ref), (ta_hbm, ta_ref), (wo_hbm, wo_ref)))
    ]
    for c in copies:
        c.start()
    height, breadth, channels = ta_ref.shape
    tiles = breadth // TILE
    rows = TILE * TILE
    total = height * breadth
    lanes = channels // 128

    slots = stage.shape[0]

    def copy(n):
        which, first = plan[n]
        return pltpu.make_async_copy(arrays[which].at[pl.ds(first, piece_rows)], stage.at[n % slots], stage_sems.at[n % slots])

    for n in range(slots):
        copy(n).start()
    for n in range(len(plan)):
        copy(n).wait()
        x = stage[n % slots].astype(jnp.float32)
        for j in range(lanes):
            table[pl.ds(n * (piece_rows // 8), piece_rows // 8), j] = x[:, 128 * j:128 * j + 128].reshape(piece_rows // 8, 8, 128)
        if n + slots < len(plan):
            copy(n + slots).start()
    flat = table.reshape(table.shape[0] * lanes * 8, 128)
    out = res.reshape(res.shape[0] * lanes * 8, 128)

    for c in copies[:2]:
        c.wait()

    idx1, w1 = idx_ref.reshape(4 * total), w_ref.reshape(4 * total)

    def line(n, carry):
        row, col = lax.rem(n, TILE), lax.div(n, TILE) * TILE
        at0 = n * (TILE * lanes)
        for j in range(TILE):
            acc = None
            for k in range(4):
                at = k * total + row * breadth + col + j
                term = w1[at] * flat[pl.ds(idx1[at], lanes, stride=8), :]
                acc = term if acc is None else acc + term
            out[pl.ds(at0 + (j // 8) * (8 * lanes) + j % 8, lanes, stride=8), :] = acc
        return carry

    lax.fori_loop(0, tiles * TILE, line, 0)
    for c in copies[2:]:
        c.wait()

    def project(t, carry):
        r = jnp.concatenate([res[pl.ds(t * (rows // 8), rows // 8), j].reshape(rows, 128) for j in range(lanes)], axis=1)
        nr = rms_rows(r.astype(jnp.bfloat16).astype(jnp.float32), gains_ref[2:3, :]).astype(jnp.bfloat16)
        at = pl.ds(pl.multiple_of(t * rows, rows), rows)
        keys[at, :] = jnp.dot(nr, wk_ref[...], preferred_element_type=jnp.float32).astype(jnp.bfloat16)
        values[at, :] = jnp.dot(nr, wv_ref[...], preferred_element_type=jnp.float32).astype(jnp.bfloat16)
        return carry

    lax.fori_loop(0, tiles, project, 0, unroll=2)

    def attend(t, carry):
        at = pl.ds(pl.multiple_of(t * rows, rows), rows)
        qa = qa_ref[:, pl.ds(pl.multiple_of(t * TILE, TILE), TILE), :].reshape(rows, channels)
        for l0, l1 in ((0, 256), (256, 384)):
            kp, vp = keys[at, l0:l1], values[at, l0:l1]
            for q0 in range(0, rows, PART):
                mixed = attend_heads(qa[q0:q0 + PART, l0:l1], kp, vp, None)
                mix[pl.ds(pl.multiple_of(t * rows + q0, PART), PART), l0:l1] = mixed.astype(jnp.bfloat16)
        return carry

    lax.fori_loop(0, tiles, attend, 0, unroll=2)

    def finish(t, carry):
        at = pl.ds(pl.multiple_of(t * rows, rows), rows)
        cols = pl.ds(pl.multiple_of(t * TILE, TILE), TILE)
        o = jnp.dot(mix[at, :], wo_ref[...], preferred_element_type=jnp.float32)
        joined = (ta_ref[:, cols, :].reshape(rows, channels).astype(jnp.float32) + o).astype(jnp.bfloat16)
        joined_ref[:, cols, :] = joined.reshape(TILE, TILE, channels)
        normed_ref[:, cols, :] = rms_rows(joined.astype(jnp.float32), gains_ref[3:4, :]).astype(jnp.bfloat16).reshape(TILE, TILE, channels)
        return carry

    lax.fori_loop(0, tiles, finish, 0, unroll=2)
    top_ref[...] = normed_ref[0:RIM]
    bottom_ref[...] = normed_ref[height - RIM:height]
    first_group = place_ref[1] == 0
    edge_ref[...] = jnp.where(first_group, normed_ref[:, breadth - SIDE:, :], normed_ref[:, 0:SIDE, :])

def gather_call(idx, weights, place, qa, ta, gains, wk, wv, wo, pieces):
    height, breadth, channels = ta.shape
    arrays, plan = [], []
    for rows, first in pieces:
        which = [n for n, array in enumerate(arrays) if array is rows]
        plan.append((which[0] if which else len(arrays), first))
        arrays += [] if which else [rows]
    piece_rows = PIECE
    n = len(pieces)
    total = height * breadth
    lanes = channels // 128
    assert height == TILE and channels == 384
    sm = pl.BlockSpec(memory_space=pltpu.SMEM)
    anywhere = pl.BlockSpec(memory_space=pl.ANY)
    square = pltpu.VMEM((channels, channels), jnp.bfloat16)
    vm = pl.BlockSpec(memory_space=pltpu.VMEM)
    shape = jax.ShapeDtypeStruct((height, breadth, channels), jnp.bfloat16)
    rim = jax.ShapeDtypeStruct((RIM, breadth, channels), jnp.bfloat16)
    return pl.pallas_call(
        functools.partial(gather_kernel, tuple(plan), len(arrays), piece_rows),
        out_shape=(shape, shape, rim, rim, jax.ShapeDtypeStruct((height, SIDE, channels), jnp.bfloat16)),
        in_specs=[sm, vm] + [anywhere] * 3 + [pl.BlockSpec(memory_space=pltpu.HBM)] * 4 + [anywhere] * len(arrays),
        out_specs=(vm,) * 5,
        scratch_shapes=[
            pltpu.VMEM((n * piece_rows // 8, lanes, 8, 128), jnp.float32),
            pltpu.VMEM((total // 8, lanes, 8, 128), jnp.float32),
            pltpu.VMEM((total, channels), jnp.bfloat16),
            pltpu.VMEM((total, channels), jnp.bfloat16),
            pltpu.VMEM((total, channels), jnp.bfloat16),
            pltpu.SMEM(idx.shape, jnp.int32),
            pltpu.SMEM(idx.shape, jnp.float32),
            pltpu.VMEM(ta.shape, jnp.bfloat16),
            pltpu.VMEM(ta.shape, jnp.bfloat16),
            square, square, square,
            pltpu.VMEM((8, piece_rows, channels), jnp.bfloat16),
            pltpu.SemaphoreType.DMA((7,)),
            pltpu.SemaphoreType.DMA((8,)),
        ],
        compiler_params=pltpu.CompilerParams(vmem_limit_bytes=60 << 20),
        cost_estimate=pl.CostEstimate(flops=30_000_000_000, transcendentals=0, bytes_accessed=10_000_000),
    )(place, gains, idx, weights, qa, ta, wk, wv, wo, *arrays)


STEP1, STEP2 = 7, 6

def gelu(x):
    return 0.5 * x * (1.0 + jnp.tanh(0.7978845608028654 * (x + 0.044715 * (x * x * x))))

def tap_copies(src, dst, sems):
    channels = src.shape[-1]
    return [
        pltpu.make_async_copy(
            src.at[a, b], dst.at[pl.ds(a * channels, channels), pl.ds(b * channels, channels)], sems.at[3 * a + b])
        for a in range(3) for b in range(3)
    ]

def conv_rows(src, rows, count, w_ref):
    span, channels = src.shape[1], src.shape[2]
    lhs = [jnp.concatenate([src[pl.ds(row + a, count)] for a in range(3)], axis=-1) for row in rows]
    lhs = lhs[0] if len(lhs) == 1 else jnp.concatenate(lhs, axis=0)
    n = len(rows) * count * span
    y = jnp.dot(lhs.reshape(n, 3 * channels), w_ref[...], preferred_element_type=jnp.float32)
    return (pltpu.roll(y[:, :channels], 1, 0) + y[:, channels:2 * channels]
            + pltpu.roll(y[:, 2 * channels:], n - 1, 0)).reshape(len(rows) * count, span, channels)

def place_sides(field, rows, edge, place_ref, breadth):
    zero = jnp.zeros_like(edge)
    field[rows, 0:SIDE, :] = jnp.where(place_ref[1] > 0, edge, zero)
    field[rows, SIDE + breadth:, :] = jnp.where(place_ref[1] + breadth < place_ref[3], edge, zero)

def columns_inside(place_ref, span):
    col = lax.broadcasted_iota(jnp.int32, (1, span, 1), 1) + (place_ref[1] - SIDE)
    return (col >= 0) & (col < place_ref[3])

def first_kernel(step, place_ref, nc_ref, side_ref, w_hbm, inner_ref, field, w, sems):
    height, breadth, channels = nc_ref.shape
    span = field.shape[1]
    copies = tap_copies(w_hbm, w, sems)
    for c in copies:
        c.start()
    field[:, SIDE:SIDE + breadth, :] = nc_ref[...]
    place_sides(field, slice(0, height), side_ref[...], place_ref, breadth)
    ok = columns_inside(place_ref, span)
    for c in copies:
        c.wait()

    def rows(n, carry):
        x = gelu(conv_rows(field, (n * step,), step, w))
        inner_ref[pl.ds(n * step, step)] = jnp.where(ok, x, 0.0).astype(jnp.bfloat16)
        return carry

    lax.fori_loop(0, (height - 2) // step, rows, 0)

def second_kernel(step, inner_ref, joined_ref, w_hbm, out_ref, w, sems):
    height, breadth, channels = joined_ref.shape
    copies = tap_copies(w_hbm, w, sems)
    for c in copies:
        c.start()
    for c in copies:
        c.wait()

    def rows(n, carry):
        y = conv_rows(inner_ref, (n * step,), step, w)[:, SIDE:SIDE + breadth, :]
        at = pl.ds(n * step + RIM, step)
        out_ref[at] = (joined_ref[at].astype(jnp.float32) + y).astype(jnp.bfloat16)
        return carry

    lax.fori_loop(0, (height - 2 * RIM) // step, rows, 0)

def rim_kernel(place_ref, nc_ref, side_ref, top_ref, bottom_ref, side_rim_ref, inner_ref, joined_ref,
               w1_hbm, w2_hbm, merged_hbm, out_hbm, field, inner, done, w1, w2, sems1, sems2, out_sems):
    height, breadth, channels = joined_ref.shape
    span = field.shape[1]
    copies1, copies2 = tap_copies(w1_hbm, w1, sems1), tap_copies(w2_hbm, w2, sems2)
    for c in copies1 + copies2:
        c.start()
    ok = columns_inside(place_ref, span)
    for c in copies1:
        c.wait()
    for end in range(2):
        own = 0 if end == 0 else height - RIM
        at = 2 * RIM * end
        own_at, far_at = (at + RIM, at) if end == 0 else (at, at + RIM)
        far = top_ref if end == 0 else bottom_ref
        field[own_at:own_at + RIM, SIDE:SIDE + breadth, :] = nc_ref[own:own + RIM]
        place_sides(field, slice(own_at, own_at + RIM), side_ref[own:own + RIM], place_ref, breadth)
        field[far_at:far_at + RIM, SIDE:SIDE + breadth, :] = far[...]
        place_sides(field, slice(far_at, far_at + RIM), side_rim_ref[end * RIM:end * RIM + RIM], place_ref, breadth)
    x = gelu(conv_rows(field, (0, 2 * RIM), RIM, w1))
    n = lax.broadcasted_iota(jnp.int32, (2 * RIM, 1, 1), 0)
    row = place_ref[0] + n + jnp.where(n < RIM, -1, height - 1 - RIM)
    x = jnp.where((row >= 0) & (row < place_ref[2]) & ok, x, 0.0).astype(jnp.bfloat16)
    inner[0:RIM] = x[:RIM]
    inner[RIM:2 * RIM] = inner_ref[0:RIM]
    inner[2 * RIM:3 * RIM] = inner_ref[height - 2 - RIM:height - 2]
    inner[3 * RIM:4 * RIM] = x[RIM:]
    for c in copies2:
        c.wait()
    y = conv_rows(inner, (0, 2 * RIM), RIM, w2)[:, SIDE:SIDE + breadth, :]
    stores = []
    for end in range(2):
        own = 0 if end == 0 else height - RIM
        done[end] = (joined_ref[own:own + RIM].astype(jnp.float32) + y[end * RIM:end * RIM + RIM]).astype(jnp.bfloat16)
        stores.append(pltpu.make_async_copy(done.at[end], out_hbm.at[pl.ds(own, RIM)], out_sems.at[end]))
        stores[end].start()
    for c in stores:
        c.wait()

SM = pl.BlockSpec(memory_space=pltpu.SMEM)
VM = pl.BlockSpec(memory_space=pltpu.VMEM)
HB = pl.BlockSpec(memory_space=pl.ANY)

def first_call(place, nc, side, w1):
    height, breadth, channels = nc.shape
    span = breadth + 2 * SIDE
    return pl.pallas_call(
        functools.partial(first_kernel, STEP1),
        out_shape=jax.ShapeDtypeStruct((height - 2, span, channels), jnp.bfloat16),
        in_specs=[SM, VM, VM, HB],
        out_specs=VM,
        scratch_shapes=[
            pltpu.VMEM((height, span, channels), jnp.bfloat16),
            pltpu.VMEM((3 * channels, 3 * channels), jnp.bfloat16),
            pltpu.SemaphoreType.DMA((9,)),
        ],
        compiler_params=pltpu.CompilerParams(vmem_limit_bytes=40 << 20),
        cost_estimate=pl.CostEstimate(flops=10_000_000_000, transcendentals=0, bytes_accessed=4_000_000),
    )(place, nc, side, w1)

def second_call(inner, joined, w2):
    channels = joined.shape[-1]
    return pl.pallas_call(
        functools.partial(second_kernel, STEP2),
        out_shape=jax.ShapeDtypeStruct(joined.shape, jnp.bfloat16),
        in_specs=[VM, VM, HB],
        out_specs=VM,
        scratch_shapes=[pltpu.VMEM((3 * channels, 3 * channels), jnp.bfloat16), pltpu.SemaphoreType.DMA((9,))],
        compiler_params=pltpu.CompilerParams(vmem_limit_bytes=40 << 20),
        cost_estimate=pl.CostEstimate(flops=8_000_000_000, transcendentals=0, bytes_accessed=4_000_000),
    )(inner, joined, w2)

def rim_call(place, nc, side, top, bottom, side_rim, inner, joined, w1, w2, merged):
    height, breadth, channels = nc.shape
    span = breadth + 2 * SIDE
    return pl.pallas_call(
        rim_kernel,
        out_shape=jax.ShapeDtypeStruct(joined.shape, jnp.bfloat16),
        in_specs=[SM] + [VM] * 7 + [HB] * 3,
        out_specs=HB,
        input_output_aliases={10: 0},
        scratch_shapes=[
            pltpu.VMEM((4 * RIM, span, channels), jnp.bfloat16),
            pltpu.VMEM((4 * RIM, span, channels), jnp.bfloat16),
            pltpu.VMEM((2, RIM, breadth, channels), jnp.bfloat16),
            pltpu.VMEM((3 * channels, 3 * channels), jnp.bfloat16),
            pltpu.VMEM((3 * channels, 3 * channels), jnp.bfloat16),
            pltpu.SemaphoreType.DMA((9,)),
            pltpu.SemaphoreType.DMA((9,)),
            pltpu.SemaphoreType.DMA((2,)),
        ],
        compiler_params=pltpu.CompilerParams(vmem_limit_bytes=40 << 20),
        cost_estimate=pl.CostEstimate(flops=5_000_000_000, transcendentals=0, bytes_accessed=4_000_000),
    )(place, nc, side, top, bottom, side_rim, inner, joined, w1, w2, merged)

def pack_kernel(place_ref, rows_ref, count_ref, keep_ref, give_ref):
    swath, group, groups = place_ref[4], place_ref[5], place_ref[6]
    peers, cap = rows_ref.shape
    lines = cap // 128
    for step in range(3):
        near = jnp.clip(swath + step - 1, 0, peers // groups - 1) * groups
        for ref, at in ((keep_ref, near + group), (give_ref, near + 1 - group)):
            row = rows_ref[pl.ds(at, 1), :]
            for n in range(lines):
                ref[step, n:n + 1, :] = row[:, 128 * n:128 * n + 128]
            ref[step, lines:lines + 1, :] = jnp.full((1, 128), count_ref[0, at], jnp.int32)


def pack_call(place, rows, count):
    sm = pl.BlockSpec(memory_space=pltpu.SMEM)
    vm = pl.BlockSpec(memory_space=pltpu.VMEM)
    shape = jax.ShapeDtypeStruct((3, rows.shape[1] // 128 + 1, 128), jnp.int32)
    return pl.pallas_call(
        pack_kernel, out_shape=(shape, shape), in_specs=[sm, vm, sm], out_specs=(vm, vm),
        cost_estimate=pl.CostEstimate(flops=1_000_000, transcendentals=0, bytes_accessed=100_000),
    )(place, rows, count)


def index_kernel(place_ref, slots_ref, weights_ref, upper_ref, keep_ref, taken_ref, lower_ref, index_ref, live_ref):
    swath, group, groups, cap, block = (place_ref[n] for n in range(4, 9))
    lines = keep_ref.shape[1] - 1
    blocks = ((upper_ref, 0), (upper_ref, 1), (keep_ref, 1), (taken_ref, 1), (lower_ref, 0), (lower_ref, 1))
    slots = slots_ref[...]
    peer, place = lax.div(slots, cap), lax.rem(slots, cap)
    step = lax.div(peer, groups) - swath
    other = jnp.where(lax.rem(peer, groups) == group, 0, 1)
    source = (step + 1) * 2 + other
    line, lane = source * lines + lax.div(place, 128), lax.rem(place, 128)
    cell = jnp.zeros_like(slots)
    count = jnp.zeros_like(slots)
    for s, (ref, at) in enumerate(blocks):
        count = jnp.where(source == s, jnp.broadcast_to(ref[at, lines:lines + 1, :], slots.shape), count)
        for n in range(lines):
            row = jnp.broadcast_to(ref[at, n:n + 1, :], slots.shape)
            picked = jnp.take_along_axis(row, lane, axis=1)
            cell = jnp.where(line == s * lines + n, picked, cell)
    toward = jnp.where(lax.rem(swath, 2) == 0, 1, -1)
    slot = jnp.where(step == 0, 0, jnp.where(step == toward, 1, 2))
    row = (slot * 2 + other) * block + cell
    index_ref[...] = lax.div(row, 8) * (8 * 3) + lax.rem(row, 8)
    live_ref[...] = jnp.where(place < count, weights_ref[...], 0.0)


def index_call(place, slots, weights, tables):
    sm = pl.BlockSpec(memory_space=pltpu.SMEM)
    vm = pl.BlockSpec(memory_space=pltpu.VMEM)
    return pl.pallas_call(
        index_kernel,
        out_shape=(jax.ShapeDtypeStruct(slots.shape, jnp.int32), jax.ShapeDtypeStruct(slots.shape, jnp.float32)),
        in_specs=[sm] + [vm] * 6,
        out_specs=(vm, vm),
        cost_estimate=pl.CostEstimate(flops=1_000_000, transcendentals=0, bytes_accessed=100_000),
    )(place, slots, weights, *tables)


def query_kernel(tokens_ref, gains_ref, w_ref, out_ref):
    height, breadth, channels = tokens_ref.shape
    for r in range(0, height, 4):
        x = rms_rows(tokens_ref[r:r + 4].reshape(4 * breadth, channels).astype(jnp.float32), gains_ref[1:2, :]).astype(jnp.bfloat16)
        q = jnp.dot(x, w_ref[...], preferred_element_type=jnp.float32).astype(jnp.bfloat16)
        out_ref[r:r + 4] = (q * jnp.bfloat16(HD ** -0.5)).reshape(4, breadth, channels)


def query_call(tokens, gains, w):
    return pl.pallas_call(
        query_kernel,
        out_shape=jax.ShapeDtypeStruct(tokens.shape, jnp.bfloat16),
        in_specs=[VM] * 3,
        out_specs=VM,
        compiler_params=pltpu.CompilerParams(vmem_limit_bytes=32 << 20),
        cost_estimate=pl.CostEstimate(flops=1_000_000, transcendentals=0, bytes_accessed=4_000_000),
    )(tokens, gains, w)


def body(
    tokens_b,
    tokens_a,
    pack_rows,
    pack_count,
    gather_slots,
    blend_weights,
    swath_gain,
    swath_query,
    swath_key,
    swath_value,
    swath_out,
    query_gain,
    source_gain,
    cross_query,
    cross_key,
    cross_value,
    cross_out,
    conv_gain,
    conv_first,
    conv_second,
):
    height, breadth, channels = tokens_b.shape
    swaths, groups = lax.axis_size("swath"), lax.axis_size("group")
    swath, group = lax.axis_index("swath"), lax.axis_index("group")
    assert groups == 2 and swaths % 2 == 0
    whole = [height * swaths, breadth * groups]
    down = [(i, i + 1) for i in range(swaths - 1)]
    up = [(j, i) for i, j in down]
    swap = [(0, 1), (1, 0)]
    pairs = [(i, i ^ 1) for i in range(swaths)]
    relay = [(i, j) for i in range(swaths) for j in [i + 2 if i % 2 == 0 else i - 2] if 0 <= j < swaths]

    def inner_edge(field):
        start = (1 - group) * (breadth - SIDE)
        return lax.dynamic_slice_in_dim(field, start, SIDE, axis=1)

    def after(values, *results):
        return lax.optimization_barrier((values, *results))[0]

    cap = pack_rows.shape[-1]
    place = jnp.stack([
        swath * height, group * breadth, jnp.int32(whole[0]), jnp.int32(whole[1]),
        swath, group, jnp.int32(groups), jnp.int32(cap), jnp.int32(height * breadth),
    ]).astype(jnp.int32)
    row = lax.broadcasted_iota(jnp.int32, (8, channels), 0)
    gains = sum(jnp.where(row == n, gain[None, :], 0.0) for n, gain in enumerate((swath_gain, query_gain, source_gain, conv_gain)))

    margin = 3
    side = lax.ppermute(inner_edge(tokens_b), "group", swap)
    top = lax.ppermute(tokens_b[height - margin:], "swath", down)
    bottom = lax.ppermute(tokens_b[:margin], "swath", up)
    projections = (swath_query, swath_key, swath_value, swath_out)

    def near(rows):
        return lax.ppermute(rows, "swath", pairs)

    def far(rows):
        return lax.ppermute(rows, "swath", relay)

    r0, r1, r2, r3 = range(0, height, ROWS)
    middle = window_call(place, gains, *projections, ((r1, 0), (r2, ROWS)), [(tokens_b, side, r1 - margin, r1 - margin, SPAN + ROWS)])
    near_middle = near(middle)
    rims = after(jnp.concatenate([top, bottom], axis=0), middle)
    rims = lax.ppermute(inner_edge(rims), "group", swap)
    ends = window_call(
        after(place, middle), gains, *projections, ((r0, 0), (r3, SPAN)),
        [(top, rims, 0, 0, margin), (tokens_b, side, 0, 0, SPAN - margin),
         (tokens_b, side, r3 - margin, r3 - margin, SPAN - margin), (bottom, rims, 0, margin, margin)],
    )
    near_ends = near(ends)

    pack_rows, pack_count = after((pack_rows, pack_count), near_ends)
    keep, give = pack_call(place, pack_rows.reshape(-1, cap), pack_count.reshape(1, -1))
    taken = lax.ppermute(give, "group", swap)
    upper = lax.ppermute(jnp.concatenate([keep[2:], taken[2:]], axis=0), "swath", down)
    lower = lax.ppermute(jnp.concatenate([keep[:1], taken[:1]], axis=0), "swath", up)
    tokens_a = after(tokens_a, ends)
    index, live = index_call(
        place, gather_slots.reshape(-1, 128), blend_weights.reshape(-1, 128), (upper, keep, taken, lower)
    )
    query_a = query_call(tokens_a, gains, cross_query)

    far_middle = far(near_middle)
    near_ends, query_a = lax.optimization_barrier((near_ends, query_a))
    far_ends = far(near_ends)
    swapped = lambda rows: lax.ppermute(rows, "group", swap)
    blocks = [(middle, ends), (swapped(middle), swapped(ends)), (near_middle, near_ends)]
    blocks += [(swapped(near_middle), swapped(after(near_ends, index, live)))]
    others = (swapped(after(far_middle, index, live)), swapped(far_ends))
    blocks += [(far_middle, far_ends), others]
    size = ROWS * breadth
    pieces = [piece for m, e in blocks for piece in ((e, 0), (m, 0), (m, size), (e, size))]
    joined, normed_c, first_rows, last_rows, edge = gather_call(
        index, live, place, query_a, tokens_a, gains,
        cross_key, cross_value, cross_out, pieces,
    )

    side = lax.ppermute(edge, "group", swap)
    top = lax.ppermute(last_rows, "swath", down)
    bottom = lax.ppermute(first_rows, "swath", up)
    inner = first_call(place, normed_c, side, conv_first)
    rims = after(jnp.concatenate([top, bottom], axis=0), inner)
    rims = lax.ppermute(inner_edge(rims), "group", swap)
    merged = second_call(inner, joined, conv_second)
    return rim_call(place, normed_c, side, top, bottom, rims, inner, joined, conv_first, conv_second, merged)


def solution(mesh):
    rows = P(("strip", "swath"), "group", None)
    maps = P(None, ("strip", "swath"), "group")
    placed = (rows, rows, P(("strip", "swath"), "group", None, None), rows, maps, maps) + (P(),) * 14
    return jax.shard_map(body, mesh=mesh, in_specs=placed, out_specs=rows, check_vma=False)
```

```python
import functools

import jax
import jax.numpy as jnp
import numpy as np
from jax import lax
from jax.experimental import pallas as pl
from jax.experimental.pallas import tpu as pltpu
from jax.sharding import PartitionSpec as P


EPSILON = 1e-06
ROWS = 4
SPAN = ROWS + 6
QC = 16
KC = 24
HD = 64

def rms_rows(x, gain):
    inv = lax.rsqrt(jnp.mean(x * x, axis=-1, keepdims=True) + EPSILON)
    return x * inv * gain

def attend_heads(q, k, v, bias):
    rows, lanes = q.shape
    heads = lanes // HD
    lane = lax.broadcasted_iota(jnp.int32, q.shape, 1) // HD
    zero = jnp.zeros_like(q)
    stacked = jnp.concatenate([jnp.where(lane == h, q, zero) for h in range(heads)], axis=0)
    s = lax.dot_general(stacked, k, (((1,), (1,)), ((), ())), preferred_element_type=jnp.float32)
    if bias is not None:
        s = s + jnp.concatenate([bias] * heads, axis=0)
    p = jnp.exp(s - jnp.max(s, axis=-1, keepdims=True))
    total = 1.0 / jnp.sum(p, axis=-1, keepdims=True)
    o = jnp.dot(p.astype(jnp.bfloat16), v, preferred_element_type=jnp.float32)
    mixed, scale = o[:rows], total[:rows]
    for h in range(1, heads):
        mixed = jnp.where(lane == h, o[h * rows:(h + 1) * rows], mixed)
        scale = jnp.where(lane == h, total[h * rows:(h + 1) * rows], scale)
    return mixed * scale

def window_kernel(spans, plan, place_ref, gain_ref, wq_hbm, wk_hbm, wv_hbm, wo_hbm, *rest):
    assert len(spans) == 2 and spans[0][1] == 0
    n_src = len(plan)
    srcs, edges = rest[:n_src], rest[n_src:2 * n_src]
    out_ref, tok, side, normed, qs, kv, mix, inside, wq, wk, wv, wo, sems = rest[2 * n_src:]
    key_rows, breadth, channels = tok.shape
    wide = normed.shape[1]
    rows = ROWS * len(spans)
    copies = []
    for n, (dst0, src0, edge0, count) in enumerate(plan):
        copies.append(pltpu.make_async_copy(edges[n].at[pl.ds(edge0, count)], side.at[pl.ds(dst0, count)], sems.at[4 + 2 * n]))
        copies.append(pltpu.make_async_copy(srcs[n].at[pl.ds(src0, count)], tok.at[pl.ds(dst0, count)], sems.at[5 + 2 * n]))
    weights = [
        pltpu.make_async_copy(src, dst, sems.at[n])
        for n, (src, dst) in enumerate(((wq_hbm, wq), (wk_hbm, wk), (wv_hbm, wv), (wo_hbm, wo)))
    ]
    for c in copies + weights:
        c.start()
    gain = gain_ref[...].reshape(1, -1)
    normed[:, breadth:, :] = jnp.zeros((key_rows, wide - breadth, channels), jnp.float32)
    n = lax.broadcasted_iota(jnp.int32, (1, SPAN * KC), 1)
    key_row = (n * 2731) >> 16
    key_col = n - key_row * KC
    m = lax.broadcasted_iota(jnp.int32, (ROWS * QC, 1), 0)
    row_gap, col_gap = key_row - (m >> 4), key_col - (m & 15)
    near = (row_gap >= 0) & (row_gap <= 6) & (col_gap >= 0) & (col_gap <= 6)
    row0, col0, height, width = place_ref[0], place_ref[1], place_ref[2], place_ref[3]
    for c in copies:
        c.wait()
    for r in range(key_rows):
        x = rms_rows(tok[r].astype(jnp.float32), gain)
        normed[r, 3:3 + breadth, :] = x
        for n_span, (_, key0) in enumerate(spans):
            if key0 + 3 <= r < key0 + 3 + ROWS:
                qs[n_span * ROWS + r - key0 - 3] = x.astype(jnp.bfloat16)
        x = rms_rows(side[r].astype(jnp.float32), gain)
        normed[r, 0:3, :] = x[5:8]
        normed[r, 3 + breadth:6 + breadth, :] = x[0:3]
    for c in weights:
        c.wait()
    q = jnp.dot(qs[...].reshape(rows * breadth, channels), wq[...], preferred_element_type=jnp.float32)
    qs[...] = (q.astype(jnp.bfloat16) * jnp.bfloat16(HD ** -0.5)).reshape(rows, breadth, channels)
    flat = normed[...].reshape(key_rows * wide, channels).astype(jnp.bfloat16)
    kv[:, :, :channels] = jnp.dot(flat, wk[...], preferred_element_type=jnp.float32).reshape(key_rows, wide, channels)
    kv[:, :, channels:] = jnp.dot(flat, wv[...], preferred_element_type=jnp.float32).reshape(key_rows, wide, channels)

    for n_span, (first_row, _) in enumerate(spans):
        row_at = key_row + (row0 + first_row - 3)
        inside[n_span] = jnp.where(near & (row_at >= 0) & (row_at < height), 0.0, -jnp.inf)
    per_span = breadth // QC
    key_step = spans[1][1]

    def block(n, carry):
        span, cb = lax.div(n, per_span), lax.rem(n, per_span)
        own, keys = pl.ds(span * ROWS, ROWS), pl.ds(span * key_step, SPAN)
        c0 = pl.multiple_of(cb * QC, QC)
        col_at = key_col + (col0 + c0 - 3)
        bias = inside[span] + jnp.where((col_at >= 0) & (col_at < width), 0.0, -jnp.inf)
        for l0, l1 in ((0, 256), (256, 384)):
            qp = qs[own, pl.ds(c0, QC), l0:l1].reshape(ROWS * QC, l1 - l0)
            kp = kv[keys, pl.ds(c0, KC), l0:l1].reshape(SPAN * KC, l1 - l0).astype(jnp.bfloat16)
            vp = kv[keys, pl.ds(c0, KC), channels + l0:channels + l1].reshape(SPAN * KC, l1 - l0).astype(jnp.bfloat16)
            mixed = attend_heads(qp, kp, vp, bias)
            mix[own, pl.ds(c0, QC), l0:l1] = mixed.astype(jnp.bfloat16).reshape(ROWS, QC, l1 - l0)
        return carry

    lax.fori_loop(0, len(spans) * per_span, block, 0, unroll=8)
    out = jnp.dot(mix[...].reshape(rows * breadth, channels), wo[...], preferred_element_type=jnp.float32)
    base = jnp.concatenate([tok[key0 + 3:key0 + 3 + ROWS] for _, key0 in spans], axis=0)
    out_ref[...] = (base.astype(jnp.float32).reshape(rows * breadth, channels) + out).astype(jnp.bfloat16)

def window_call(place, gains, wq, wk, wv, wo, spans, parts):
    plan, srcs, edges, at = [], [], [], 0
    for array, edge, first, edge_first, count in parts:
        plan.append((at, first, edge_first, count))
        srcs.append(array)
        edges.append(edge)
        at += count
    breadth, channels = srcs[0].shape[1:]
    wide = breadth + 8
    rows = ROWS * len(spans)
    square = pltpu.VMEM((channels, channels), jnp.bfloat16)
    return pl.pallas_call(
        functools.partial(window_kernel, tuple(spans), tuple(plan)),
        out_shape=jax.ShapeDtypeStruct((rows * breadth, channels), jnp.bfloat16),
        in_specs=[pl.BlockSpec(memory_space=pltpu.SMEM), pl.BlockSpec(memory_space=pltpu.VMEM)]
        + [pl.BlockSpec(memory_space=pltpu.HBM)] * 4 + [pl.BlockSpec(memory_space=pl.ANY)] * (2 * len(srcs)),
        out_specs=pl.BlockSpec(memory_space=pltpu.VMEM),
        scratch_shapes=[
            pltpu.VMEM((at, breadth, channels), jnp.bfloat16),
            pltpu.VMEM((at, 8, channels), jnp.bfloat16),
            pltpu.VMEM((at, wide, channels), jnp.float32),
            pltpu.VMEM((rows, breadth, channels), jnp.bfloat16),
            pltpu.VMEM((at, wide, 2 * channels), jnp.float32),
            pltpu.VMEM((rows, breadth, channels), jnp.bfloat16),
            pltpu.VMEM((len(spans), ROWS * QC, SPAN * KC), jnp.float32),
            square, square, square, square,
            pltpu.SemaphoreType.DMA((4 + 2 * len(srcs),)),
        ],
        compiler_params=pltpu.CompilerParams(vmem_limit_bytes=60 << 20),
        cost_estimate=pl.CostEstimate(flops=14_000_000_000, transcendentals=0, bytes_accessed=4_000_000),
    )(place, gains, wq, wk, wv, wo, *srcs, *edges)


TILE = 16
PART = 64
BATCH = 4
RIM = 2
SIDE = 8
PIECE = 512

def gather_kernel(plan, n_arrays, piece_rows, *refs):
    place_ref, gains_ref, idx_hbm, w_hbm, qa_hbm, ta_hbm, wk_hbm, wv_hbm, wo_hbm = refs[:9]
    arrays = refs[9:9 + n_arrays]
    (joined_ref, normed_ref, top_ref, bottom_ref, edge_ref, table, res, mix,
     idx_ref, w_ref, qa_ref, ta_ref, wk_ref, wv_ref, wo_ref, stage, sems, stage_sems) = refs[9 + n_arrays:]
    copies = [
        pltpu.make_async_copy(src, dst, sems.at[n])
        for n, (src, dst) in enumerate((
            (idx_hbm, idx_ref), (w_hbm, w_ref), (wk_hbm, wk_ref), (wv_hbm, wv_ref), (qa_hbm, qa_ref), (ta_hbm, ta_ref), (wo_hbm, wo_ref)))
    ]
    for c in copies:
        c.start()
    height, breadth, channels = ta_ref.shape
    tiles = breadth // TILE
    rows = TILE * TILE
    total = height * breadth
    lanes = channels // 128

    slots = stage.shape[0]

    def copy(n):
        which, first = plan[n]
        return pltpu.make_async_copy(arrays[which].at[pl.ds(first, piece_rows)], stage.at[n % slots], stage_sems.at[n % slots])

    for n in range(slots):
        copy(n).start()
    for n in range(len(plan)):
        copy(n).wait()
        x = stage[n % slots].astype(jnp.float32)
        for j in range(lanes):
            table[pl.ds(n * (piece_rows // 8), piece_rows // 8), j] = x[:, 128 * j:128 * j + 128].reshape(piece_rows // 8, 8, 128)
        if n + slots < len(plan):
            copy(n + slots).start()
    flat = table.reshape(table.shape[0] * lanes * 8, 128)
    out = res.reshape(res.shape[0] * lanes * 8, 128)

    for c in copies[:2]:
        c.wait()

    idx1, w1 = idx_ref.reshape(4 * total), w_ref.reshape(4 * total)

    def line(tile, i):
        at0 = tile * (rows * lanes) + i * (TILE * lanes)
        base = i * breadth + tile * TILE
        for j in range(TILE):
            acc = None
            for k in range(4):
                at = base + (k * total + j)
                term = w1[at] * flat[pl.ds(idx1[at], lanes, stride=8), :]
                acc = term if acc is None else acc + term
            out[pl.ds(at0 + (j // 8) * (8 * lanes) + j % 8, lanes, stride=8), :] = acc

    def first_tile(i, carry):
        line(0, i)
        return carry

    lax.fori_loop(0, TILE, first_tile, 0)
    for c in copies[2:]:
        c.wait()

    def attend(t, carry):
        r = jnp.concatenate([res[pl.ds(t * (rows // 8), rows // 8), j].reshape(rows, 128) for j in range(lanes)], axis=1)
        nr = rms_rows(r.astype(jnp.bfloat16).astype(jnp.float32), gains_ref[2:3, :]).astype(jnp.bfloat16)
        kk = jnp.dot(nr, wk_ref[...], preferred_element_type=jnp.float32).astype(jnp.bfloat16)
        vv = jnp.dot(nr, wv_ref[...], preferred_element_type=jnp.float32).astype(jnp.bfloat16)
        qa = qa_ref[:, pl.ds(pl.multiple_of(t * TILE, TILE), TILE), :].reshape(rows, channels)
        following = jnp.minimum(t + 1, tiles - 1)
        units = [(l0, l1, q0) for l0, l1 in ((0, 256), (256, 384)) for q0 in range(0, rows, PART)]
        per = TILE // len(units)
        for n, (l0, l1, q0) in enumerate(units):
            mixed = attend_heads(qa[q0:q0 + PART, l0:l1], kk[:, l0:l1], vv[:, l0:l1], None)
            mix[pl.ds(pl.multiple_of(t * rows + q0, PART), PART), l0:l1] = mixed.astype(jnp.bfloat16)
            for i in range(n * per, n * per + per):
                line(following, i)
        return carry

    lax.fori_loop(0, tiles, attend, 0)

    def finish(t, carry):
        at = pl.ds(pl.multiple_of(t * (BATCH * rows), rows), BATCH * rows)
        o = jnp.dot(mix[at, :], wo_ref[...], preferred_element_type=jnp.float32)
        for n in range(BATCH):
            cols = pl.ds(pl.multiple_of((t * BATCH + n) * TILE, TILE), TILE)
            joined = (ta_ref[:, cols, :].reshape(rows, channels).astype(jnp.float32) + o[n * rows:(n + 1) * rows]).astype(jnp.bfloat16)
            joined_ref[:, cols, :] = joined.reshape(TILE, TILE, channels)
            normed_ref[:, cols, :] = rms_rows(joined.astype(jnp.float32), gains_ref[3:4, :]).astype(jnp.bfloat16).reshape(TILE, TILE, channels)
        return carry

    lax.fori_loop(0, tiles // BATCH, finish, 0)
    top_ref[...] = normed_ref[0:RIM]
    bottom_ref[...] = normed_ref[height - RIM:height]
    first_group = place_ref[1] == 0
    edge_ref[...] = jnp.where(first_group, normed_ref[:, breadth - SIDE:, :], normed_ref[:, 0:SIDE, :])

def gather_call(idx, weights, place, qa, ta, gains, wk, wv, wo, pieces):
    height, breadth, channels = ta.shape
    arrays, plan = [], []
    for rows, first in pieces:
        which = [n for n, array in enumerate(arrays) if array is rows]
        plan.append((which[0] if which else len(arrays), first))
        arrays += [] if which else [rows]
    piece_rows = PIECE
    n = len(pieces)
    total = height * breadth
    lanes = channels // 128
    assert height == TILE and channels == 384
    sm = pl.BlockSpec(memory_space=pltpu.SMEM)
    anywhere = pl.BlockSpec(memory_space=pl.ANY)
    square = pltpu.VMEM((channels, channels), jnp.bfloat16)
    vm = pl.BlockSpec(memory_space=pltpu.VMEM)
    shape = jax.ShapeDtypeStruct((height, breadth, channels), jnp.bfloat16)
    rim = jax.ShapeDtypeStruct((RIM, breadth, channels), jnp.bfloat16)
    return pl.pallas_call(
        functools.partial(gather_kernel, tuple(plan), len(arrays), piece_rows),
        out_shape=(shape, shape, rim, rim, jax.ShapeDtypeStruct((height, SIDE, channels), jnp.bfloat16)),
        in_specs=[sm, vm] + [anywhere] * 3 + [pl.BlockSpec(memory_space=pltpu.HBM)] * 4 + [anywhere] * len(arrays),
        out_specs=(vm,) * 5,
        scratch_shapes=[
            pltpu.VMEM((n * piece_rows // 8, lanes, 8, 128), jnp.float32),
            pltpu.VMEM((total // 8, lanes, 8, 128), jnp.float32),
            pltpu.VMEM((total, channels), jnp.bfloat16),
            pltpu.SMEM(idx.shape, jnp.int32),
            pltpu.SMEM(idx.shape, jnp.float32),
            pltpu.VMEM(ta.shape, jnp.bfloat16),
            pltpu.VMEM(ta.shape, jnp.bfloat16),
            square, square, square,
            pltpu.VMEM((8, piece_rows, channels), jnp.bfloat16),
            pltpu.SemaphoreType.DMA((7,)),
            pltpu.SemaphoreType.DMA((8,)),
        ],
        compiler_params=pltpu.CompilerParams(vmem_limit_bytes=60 << 20),
        cost_estimate=pl.CostEstimate(flops=30_000_000_000, transcendentals=0, bytes_accessed=10_000_000),
    )(place, gains, idx, weights, qa, ta, wk, wv, wo, *arrays)


STEP1, STEP2 = 7, 6

def gelu(x):
    return 0.5 * x * (1.0 + jnp.tanh(0.7978845608028654 * (x + 0.044715 * (x * x * x))))

def tap_copies(src, dst, sems):
    channels = src.shape[-1]
    return [
        pltpu.make_async_copy(
            src.at[a, b], dst.at[pl.ds(a * channels, channels), pl.ds(b * channels, channels)], sems.at[3 * a + b])
        for a in range(3) for b in range(3)
    ]

def conv_rows(src, rows, count, w_ref):
    span, channels = src.shape[1], src.shape[2]
    lhs = [jnp.concatenate([src[pl.ds(row + a, count)] for a in range(3)], axis=-1) for row in rows]
    lhs = lhs[0] if len(lhs) == 1 else jnp.concatenate(lhs, axis=0)
    n = len(rows) * count * span
    y = jnp.dot(lhs.reshape(n, 3 * channels), w_ref[...], preferred_element_type=jnp.float32)
    return (pltpu.roll(y[:, :channels], 1, 0) + y[:, channels:2 * channels]
            + pltpu.roll(y[:, 2 * channels:], n - 1, 0)).reshape(len(rows) * count, span, channels)

def place_sides(field, rows, edge, place_ref, breadth):
    zero = jnp.zeros_like(edge)
    field[rows, 0:SIDE, :] = jnp.where(place_ref[1] > 0, edge, zero)
    field[rows, SIDE + breadth:, :] = jnp.where(place_ref[1] + breadth < place_ref[3], edge, zero)

def columns_inside(place_ref, span):
    col = lax.broadcasted_iota(jnp.int32, (1, span, 1), 1) + (place_ref[1] - SIDE)
    return (col >= 0) & (col < place_ref[3])

def first_kernel(step, place_ref, nc_ref, side_ref, w_hbm, inner_ref, field, w, sems):
    height, breadth, channels = nc_ref.shape
    span = field.shape[1]
    copies = tap_copies(w_hbm, w, sems)
    for c in copies:
        c.start()
    field[:, SIDE:SIDE + breadth, :] = nc_ref[...]
    place_sides(field, slice(0, height), side_ref[...], place_ref, breadth)
    ok = columns_inside(place_ref, span)
    for c in copies:
        c.wait()

    def rows(n, carry):
        x = gelu(conv_rows(field, (n * step,), step, w))
        inner_ref[pl.ds(n * step, step)] = jnp.where(ok, x, 0.0).astype(jnp.bfloat16)
        return carry

    lax.fori_loop(0, (height - 2) // step, rows, 0)

def second_kernel(step, inner_ref, joined_ref, w_hbm, out_ref, w, sems):
    height, breadth, channels = joined_ref.shape
    copies = tap_copies(w_hbm, w, sems)
    for c in copies:
        c.start()
    for c in copies:
        c.wait()

    def rows(n, carry):
        y = conv_rows(inner_ref, (n * step,), step, w)[:, SIDE:SIDE + breadth, :]
        at = pl.ds(n * step + RIM, step)
        out_ref[at] = (joined_ref[at].astype(jnp.float32) + y).astype(jnp.bfloat16)
        return carry

    lax.fori_loop(0, (height - 2 * RIM) // step, rows, 0)

def rim_kernel(place_ref, nc_ref, side_ref, top_ref, bottom_ref, side_rim_ref, inner_ref, joined_ref,
               w1_hbm, w2_hbm, merged_hbm, out_hbm, field, inner, done, w1, w2, sems1, sems2, out_sems):
    height, breadth, channels = joined_ref.shape
    span = field.shape[1]
    copies1, copies2 = tap_copies(w1_hbm, w1, sems1), tap_copies(w2_hbm, w2, sems2)
    for c in copies1 + copies2:
        c.start()
    ok = columns_inside(place_ref, span)
    for c in copies1:
        c.wait()
    for end in range(2):
        own = 0 if end == 0 else height - RIM
        at = 2 * RIM * end
        own_at, far_at = (at + RIM, at) if end == 0 else (at, at + RIM)
        far = top_ref if end == 0 else bottom_ref
        field[own_at:own_at + RIM, SIDE:SIDE + breadth, :] = nc_ref[own:own + RIM]
        place_sides(field, slice(own_at, own_at + RIM), side_ref[own:own + RIM], place_ref, breadth)
        field[far_at:far_at + RIM, SIDE:SIDE + breadth, :] = far[...]
        place_sides(field, slice(far_at, far_at + RIM), side_rim_ref[end * RIM:end * RIM + RIM], place_ref, breadth)
    x = gelu(conv_rows(field, (0, 2 * RIM), RIM, w1))
    n = lax.broadcasted_iota(jnp.int32, (2 * RIM, 1, 1), 0)
    row = place_ref[0] + n + jnp.where(n < RIM, -1, height - 1 - RIM)
    x = jnp.where((row >= 0) & (row < place_ref[2]) & ok, x, 0.0).astype(jnp.bfloat16)
    inner[0:RIM] = x[:RIM]
    inner[RIM:2 * RIM] = inner_ref[0:RIM]
    inner[2 * RIM:3 * RIM] = inner_ref[height - 2 - RIM:height - 2]
    inner[3 * RIM:4 * RIM] = x[RIM:]
    for c in copies2:
        c.wait()
    y = conv_rows(inner, (0, 2 * RIM), RIM, w2)[:, SIDE:SIDE + breadth, :]
    stores = []
    for end in range(2):
        own = 0 if end == 0 else height - RIM
        done[end] = (joined_ref[own:own + RIM].astype(jnp.float32) + y[end * RIM:end * RIM + RIM]).astype(jnp.bfloat16)
        stores.append(pltpu.make_async_copy(done.at[end], out_hbm.at[pl.ds(own, RIM)], out_sems.at[end]))
        stores[end].start()
    for c in stores:
        c.wait()

SM = pl.BlockSpec(memory_space=pltpu.SMEM)
VM = pl.BlockSpec(memory_space=pltpu.VMEM)
HB = pl.BlockSpec(memory_space=pl.ANY)

def first_call(place, nc, side, w1):
    height, breadth, channels = nc.shape
    span = breadth + 2 * SIDE
    return pl.pallas_call(
        functools.partial(first_kernel, STEP1),
        out_shape=jax.ShapeDtypeStruct((height - 2, span, channels), jnp.bfloat16),
        in_specs=[SM, VM, VM, HB],
        out_specs=VM,
        scratch_shapes=[
            pltpu.VMEM((height, span, channels), jnp.bfloat16),
            pltpu.VMEM((3 * channels, 3 * channels), jnp.bfloat16),
            pltpu.SemaphoreType.DMA((9,)),
        ],
        compiler_params=pltpu.CompilerParams(vmem_limit_bytes=40 << 20),
        cost_estimate=pl.CostEstimate(flops=10_000_000_000, transcendentals=0, bytes_accessed=4_000_000),
    )(place, nc, side, w1)

def second_call(inner, joined, w2):
    channels = joined.shape[-1]
    return pl.pallas_call(
        functools.partial(second_kernel, STEP2),
        out_shape=jax.ShapeDtypeStruct(joined.shape, jnp.bfloat16),
        in_specs=[VM, VM, HB],
        out_specs=VM,
        scratch_shapes=[pltpu.VMEM((3 * channels, 3 * channels), jnp.bfloat16), pltpu.SemaphoreType.DMA((9,))],
        compiler_params=pltpu.CompilerParams(vmem_limit_bytes=40 << 20),
        cost_estimate=pl.CostEstimate(flops=8_000_000_000, transcendentals=0, bytes_accessed=4_000_000),
    )(inner, joined, w2)

def rim_call(place, nc, side, top, bottom, side_rim, inner, joined, w1, w2, merged):
    height, breadth, channels = nc.shape
    span = breadth + 2 * SIDE
    return pl.pallas_call(
        rim_kernel,
        out_shape=jax.ShapeDtypeStruct(joined.shape, jnp.bfloat16),
        in_specs=[SM] + [VM] * 7 + [HB] * 3,
        out_specs=HB,
        input_output_aliases={10: 0},
        scratch_shapes=[
            pltpu.VMEM((4 * RIM, span, channels), jnp.bfloat16),
            pltpu.VMEM((4 * RIM, span, channels), jnp.bfloat16),
            pltpu.VMEM((2, RIM, breadth, channels), jnp.bfloat16),
            pltpu.VMEM((3 * channels, 3 * channels), jnp.bfloat16),
            pltpu.VMEM((3 * channels, 3 * channels), jnp.bfloat16),
            pltpu.SemaphoreType.DMA((9,)),
            pltpu.SemaphoreType.DMA((9,)),
            pltpu.SemaphoreType.DMA((2,)),
        ],
        compiler_params=pltpu.CompilerParams(vmem_limit_bytes=40 << 20),
        cost_estimate=pl.CostEstimate(flops=5_000_000_000, transcendentals=0, bytes_accessed=4_000_000),
    )(place, nc, side, top, bottom, side_rim, inner, joined, w1, w2, merged)

def pack_kernel(place_ref, rows_ref, count_ref, keep_ref, give_ref):
    swath, group, groups = place_ref[4], place_ref[5], place_ref[6]
    peers, cap = rows_ref.shape
    lines = cap // 128
    for step in range(3):
        near = jnp.clip(swath + step - 1, 0, peers // groups - 1) * groups
        for ref, at in ((keep_ref, near + group), (give_ref, near + 1 - group)):
            row = rows_ref[pl.ds(at, 1), :]
            for n in range(lines):
                ref[step, n:n + 1, :] = row[:, 128 * n:128 * n + 128]
            ref[step, lines:lines + 1, :] = jnp.full((1, 128), count_ref[0, at], jnp.int32)


def pack_call(place, rows, count):
    sm = pl.BlockSpec(memory_space=pltpu.SMEM)
    vm = pl.BlockSpec(memory_space=pltpu.VMEM)
    shape = jax.ShapeDtypeStruct((3, rows.shape[1] // 128 + 1, 128), jnp.int32)
    return pl.pallas_call(
        pack_kernel, out_shape=(shape, shape), in_specs=[sm, vm, sm], out_specs=(vm, vm),
        cost_estimate=pl.CostEstimate(flops=1_000_000, transcendentals=0, bytes_accessed=100_000),
    )(place, rows, count)


def index_kernel(place_ref, slots_ref, weights_ref, upper_ref, keep_ref, taken_ref, lower_ref, index_ref, live_ref):
    swath, group, groups, cap, block = (place_ref[n] for n in range(4, 9))
    lines = keep_ref.shape[1] - 1
    blocks = ((upper_ref, 0), (upper_ref, 1), (keep_ref, 1), (taken_ref, 1), (lower_ref, 0), (lower_ref, 1))
    slots = slots_ref[...]
    peer, place = lax.div(slots, cap), lax.rem(slots, cap)
    step = lax.div(peer, groups) - swath
    other = jnp.where(lax.rem(peer, groups) == group, 0, 1)
    source = (step + 1) * 2 + other
    line, lane = source * lines + lax.div(place, 128), lax.rem(place, 128)
    cell = jnp.zeros_like(slots)
    count = jnp.zeros_like(slots)
    for s, (ref, at) in enumerate(blocks):
        count = jnp.where(source == s, jnp.broadcast_to(ref[at, lines:lines + 1, :], slots.shape), count)
        for n in range(lines):
            row = jnp.broadcast_to(ref[at, n:n + 1, :], slots.shape)
            picked = jnp.take_along_axis(row, lane, axis=1)
            cell = jnp.where(line == s * lines + n, picked, cell)
    toward = jnp.where(lax.rem(swath, 2) == 0, 1, -1)
    slot = jnp.where(step == 0, 0, jnp.where(step == toward, 1, 2))
    row = (slot * 2 + other) * block + cell
    index_ref[...] = lax.div(row, 8) * (8 * 3) + lax.rem(row, 8)
    live_ref[...] = jnp.where(place < count, weights_ref[...], 0.0)


def index_call(place, slots, weights, tables):
    sm = pl.BlockSpec(memory_space=pltpu.SMEM)
    vm = pl.BlockSpec(memory_space=pltpu.VMEM)
    return pl.pallas_call(
        index_kernel,
        out_shape=(jax.ShapeDtypeStruct(slots.shape, jnp.int32), jax.ShapeDtypeStruct(slots.shape, jnp.float32)),
        in_specs=[sm] + [vm] * 6,
        out_specs=(vm, vm),
        cost_estimate=pl.CostEstimate(flops=1_000_000, transcendentals=0, bytes_accessed=100_000),
    )(place, slots, weights, *tables)


def query_kernel(tokens_ref, gains_ref, w_ref, out_ref):
    height, breadth, channels = tokens_ref.shape
    for r in range(0, height, 4):
        x = rms_rows(tokens_ref[r:r + 4].reshape(4 * breadth, channels).astype(jnp.float32), gains_ref[1:2, :]).astype(jnp.bfloat16)
        q = jnp.dot(x, w_ref[...], preferred_element_type=jnp.float32).astype(jnp.bfloat16)
        out_ref[r:r + 4] = (q * jnp.bfloat16(HD ** -0.5)).reshape(4, breadth, channels)


def query_call(tokens, gains, w):
    return pl.pallas_call(
        query_kernel,
        out_shape=jax.ShapeDtypeStruct(tokens.shape, jnp.bfloat16),
        in_specs=[VM] * 3,
        out_specs=VM,
        compiler_params=pltpu.CompilerParams(vmem_limit_bytes=32 << 20),
        cost_estimate=pl.CostEstimate(flops=1_000_000, transcendentals=0, bytes_accessed=4_000_000),
    )(tokens, gains, w)


def body(
    tokens_b,
    tokens_a,
    pack_rows,
    pack_count,
    gather_slots,
    blend_weights,
    swath_gain,
    swath_query,
    swath_key,
    swath_value,
    swath_out,
    query_gain,
    source_gain,
    cross_query,
    cross_key,
    cross_value,
    cross_out,
    conv_gain,
    conv_first,
    conv_second,
):
    height, breadth, channels = tokens_b.shape
    swaths, groups = lax.axis_size("swath"), lax.axis_size("group")
    swath, group = lax.axis_index("swath"), lax.axis_index("group")
    assert groups == 2 and swaths % 2 == 0
    whole = [height * swaths, breadth * groups]
    down = [(i, i + 1) for i in range(swaths - 1)]
    up = [(j, i) for i, j in down]
    swap = [(0, 1), (1, 0)]
    pairs = [(i, i ^ 1) for i in range(swaths)]
    relay = [(i, j) for i in range(swaths) for j in [i + 2 if i % 2 == 0 else i - 2] if 0 <= j < swaths]

    def inner_edge(field):
        start = (1 - group) * (breadth - SIDE)
        return lax.dynamic_slice_in_dim(field, start, SIDE, axis=1)

    def after(values, *results):
        return lax.optimization_barrier((values, *results))[0]

    cap = pack_rows.shape[-1]
    place = jnp.stack([
        swath * height, group * breadth, jnp.int32(whole[0]), jnp.int32(whole[1]),
        swath, group, jnp.int32(groups), jnp.int32(cap), jnp.int32(height * breadth),
    ]).astype(jnp.int32)

    margin = 3
    side = lax.ppermute(inner_edge(tokens_b), "group", swap)
    top = lax.ppermute(tokens_b[height - margin:], "swath", down)
    bottom = lax.ppermute(tokens_b[:margin], "swath", up)
    projections = (swath_query, swath_key, swath_value, swath_out)

    def near(rows):
        return lax.ppermute(rows, "swath", pairs)

    def far(rows):
        return lax.ppermute(rows, "swath", relay)

    r0, r1, r2, r3 = range(0, height, ROWS)
    middle = window_call(place, swath_gain, *projections, ((r1, 0), (r2, ROWS)), [(tokens_b, side, r1 - margin, r1 - margin, SPAN + ROWS)])
    near_middle = near(middle)
    row = lax.broadcasted_iota(jnp.int32, (8, channels), 0)
    gains = sum(jnp.where(row == n, gain[None, :], 0.0) for n, gain in enumerate((swath_gain, query_gain, source_gain, after(conv_gain, middle))))
    rims = after(jnp.concatenate([top, bottom], axis=0), middle)
    rims = lax.ppermute(inner_edge(rims), "group", swap)
    ends = window_call(
        after(place, middle), swath_gain, *projections, ((r0, 0), (r3, SPAN)),
        [(top, rims, 0, 0, margin), (tokens_b, side, 0, 0, SPAN - margin),
         (tokens_b, side, r3 - margin, r3 - margin, SPAN - margin), (bottom, rims, 0, margin, margin)],
    )
    near_ends = near(ends)

    pack_rows, pack_count = after((pack_rows, pack_count), near_ends)
    keep, give = pack_call(place, pack_rows.reshape(-1, cap), pack_count.reshape(1, -1))
    taken = lax.ppermute(give, "group", swap)
    upper = lax.ppermute(jnp.concatenate([keep[2:], taken[2:]], axis=0), "swath", down)
    lower = lax.ppermute(jnp.concatenate([keep[:1], taken[:1]], axis=0), "swath", up)
    tokens_a = after(tokens_a, ends)
    index, live = index_call(
        place, gather_slots.reshape(-1, 128), blend_weights.reshape(-1, 128), (upper, keep, taken, lower)
    )
    query_a = query_call(tokens_a, gains, cross_query)

    far_middle = far(near_middle)
    near_ends, query_a = lax.optimization_barrier((near_ends, query_a))
    far_ends = far(near_ends)
    swapped = lambda rows: lax.ppermute(rows, "group", swap)
    blocks = [(middle, ends), (swapped(middle), swapped(ends)), (near_middle, near_ends)]
    blocks += [(swapped(near_middle), swapped(after(near_ends, index, live)))]
    others = (swapped(after(far_middle, index, live)), swapped(far_ends))
    blocks += [(far_middle, far_ends), others]
    size = ROWS * breadth
    pieces = [piece for m, e in blocks for piece in ((e, 0), (m, 0), (m, size), (e, size))]
    joined, normed_c, first_rows, last_rows, edge = gather_call(
        index, live, place, query_a, tokens_a, gains,
        cross_key, cross_value, cross_out, pieces,
    )

    side = lax.ppermute(edge, "group", swap)
    top = lax.ppermute(last_rows, "swath", down)
    bottom = lax.ppermute(first_rows, "swath", up)
    inner = first_call(place, normed_c, side, conv_first)
    rims = after(jnp.concatenate([top, bottom], axis=0), inner)
    rims = lax.ppermute(inner_edge(rims), "group", swap)
    merged = second_call(inner, joined, conv_second)
    return rim_call(place, normed_c, side, top, bottom, rims, inner, joined, conv_first, conv_second, merged)


def solution(mesh):
    rows = P(("strip", "swath"), "group", None)
    maps = P(None, ("strip", "swath"), "group")
    placed = (rows, rows, P(("strip", "swath"), "group", None, None), rows, maps, maps) + (P(),) * 14
    return jax.shard_map(body, mesh=mesh, in_specs=placed, out_specs=rows, check_vma=False)
```

```python
import functools

import jax
import jax.numpy as jnp
import numpy as np
from jax import lax
from jax.experimental import pallas as pl
from jax.experimental.pallas import tpu as pltpu
from jax.sharding import PartitionSpec as P


EPSILON = 1e-06
ROWS = 4
SPAN = ROWS + 6
QC = 16
KC = 24
HD = 64

def rms_rows(x, gain):
    inv = lax.rsqrt(jnp.mean(x * x, axis=-1, keepdims=True) + EPSILON)
    return x * inv * gain

def attend_heads(q, k, v, bias):
    rows, lanes = q.shape
    heads = lanes // HD
    lane = lax.broadcasted_iota(jnp.int32, q.shape, 1) // HD
    zero = jnp.zeros_like(q)
    stacked = jnp.concatenate([jnp.where(lane == h, q, zero) for h in range(heads)], axis=0)
    s = lax.dot_general(stacked, k, (((1,), (1,)), ((), ())), preferred_element_type=jnp.float32)
    if bias is not None:
        s = s + jnp.concatenate([bias] * heads, axis=0)
    p = jnp.exp(s - jnp.max(s, axis=-1, keepdims=True))
    total = 1.0 / jnp.sum(p, axis=-1, keepdims=True)
    o = jnp.dot(p.astype(jnp.bfloat16), v, preferred_element_type=jnp.float32)
    mixed, scale = o[:rows], total[:rows]
    for h in range(1, heads):
        mixed = jnp.where(lane == h, o[h * rows:(h + 1) * rows], mixed)
        scale = jnp.where(lane == h, total[h * rows:(h + 1) * rows], scale)
    return mixed * scale

def window_kernel(spans, plan, place_ref, gain_ref, wq_hbm, wk_hbm, wv_hbm, wo_hbm, *rest):
    assert len(spans) == 2 and spans[0][1] == 0
    n_src = len(plan)
    srcs, edges = rest[:n_src], rest[n_src:2 * n_src]
    out_ref, tok, side, normed, qs, kv, mix, inside, wq, wk, wv, wo, sems = rest[2 * n_src:]
    key_rows, breadth, channels = tok.shape
    wide = normed.shape[1]
    rows = ROWS * len(spans)
    copies = []
    for n, (dst0, src0, edge0, count) in enumerate(plan):
        copies.append(pltpu.make_async_copy(edges[n].at[pl.ds(edge0, count)], side.at[pl.ds(dst0, count)], sems.at[4 + 2 * n]))
        copies.append(pltpu.make_async_copy(srcs[n].at[pl.ds(src0, count)], tok.at[pl.ds(dst0, count)], sems.at[5 + 2 * n]))
    weights = [
        pltpu.make_async_copy(src, dst, sems.at[n])
        for n, (src, dst) in enumerate(((wq_hbm, wq), (wk_hbm, wk), (wv_hbm, wv), (wo_hbm, wo)))
    ]
    for c in copies + weights:
        c.start()
    gain = gain_ref[...].reshape(1, -1)
    normed[:, breadth:, :] = jnp.zeros((key_rows, wide - breadth, channels), jnp.float32)
    n = lax.broadcasted_iota(jnp.int32, (1, SPAN * KC), 1)
    key_row = (n * 2731) >> 16
    key_col = n - key_row * KC
    m = lax.broadcasted_iota(jnp.int32, (ROWS * QC, 1), 0)
    row_gap, col_gap = key_row - (m >> 4), key_col - (m & 15)
    near = (row_gap >= 0) & (row_gap <= 6) & (col_gap >= 0) & (col_gap <= 6)
    row0, col0, height, width = place_ref[0], place_ref[1], place_ref[2], place_ref[3]
    for c in copies:
        c.wait()
    for r in range(key_rows):
        x = rms_rows(tok[r].astype(jnp.float32), gain)
        normed[r, 3:3 + breadth, :] = x
        for n_span, (_, key0) in enumerate(spans):
            if key0 + 3 <= r < key0 + 3 + ROWS:
                qs[n_span * ROWS + r - key0 - 3] = x.astype(jnp.bfloat16)
        x = rms_rows(side[r].astype(jnp.float32), gain)
        normed[r, 0:3, :] = x[5:8]
        normed[r, 3 + breadth:6 + breadth, :] = x[0:3]
    for c in weights:
        c.wait()
    q = jnp.dot(qs[...].reshape(rows * breadth, channels), wq[...], preferred_element_type=jnp.float32)
    qs[...] = (q.astype(jnp.bfloat16) * jnp.bfloat16(HD ** -0.5)).reshape(rows, breadth, channels)
    flat = normed[...].reshape(key_rows * wide, channels).astype(jnp.bfloat16)
    kv[:, :, :channels] = jnp.dot(flat, wk[...], preferred_element_type=jnp.float32).reshape(key_rows, wide, channels)
    kv[:, :, channels:] = jnp.dot(flat, wv[...], preferred_element_type=jnp.float32).reshape(key_rows, wide, channels)

    for n_span, (first_row, _) in enumerate(spans):
        row_at = key_row + (row0 + first_row - 3)
        inside[n_span] = jnp.where(near & (row_at >= 0) & (row_at < height), 0.0, -jnp.inf)
    per_span = breadth // QC
    key_step = spans[1][1]

    def block(n, carry):
        span, cb = lax.div(n, per_span), lax.rem(n, per_span)
        own, keys = pl.ds(span * ROWS, ROWS), pl.ds(span * key_step, SPAN)
        c0 = pl.multiple_of(cb * QC, QC)
        col_at = key_col + (col0 + c0 - 3)
        bias = inside[span] + jnp.where((col_at >= 0) & (col_at < width), 0.0, -jnp.inf)
        for l0, l1 in ((0, 256), (256, 384)):
            qp = qs[own, pl.ds(c0, QC), l0:l1].reshape(ROWS * QC, l1 - l0)
            kp = kv[keys, pl.ds(c0, KC), l0:l1].reshape(SPAN * KC, l1 - l0).astype(jnp.bfloat16)
            vp = kv[keys, pl.ds(c0, KC), channels + l0:channels + l1].reshape(SPAN * KC, l1 - l0).astype(jnp.bfloat16)
            mixed = attend_heads(qp, kp, vp, bias)
            mix[own, pl.ds(c0, QC), l0:l1] = mixed.astype(jnp.bfloat16).reshape(ROWS, QC, l1 - l0)
        return carry

    lax.fori_loop(0, len(spans) * per_span, block, 0, unroll=8)
    out = jnp.dot(mix[...].reshape(rows * breadth, channels), wo[...], preferred_element_type=jnp.float32)
    base = jnp.concatenate([tok[key0 + 3:key0 + 3 + ROWS] for _, key0 in spans], axis=0)
    out_ref[...] = (base.astype(jnp.float32).reshape(rows * breadth, channels) + out).astype(jnp.bfloat16)

def window_call(place, gains, wq, wk, wv, wo, spans, parts):
    plan, srcs, edges, at = [], [], [], 0
    for array, edge, first, edge_first, count in parts:
        plan.append((at, first, edge_first, count))
        srcs.append(array)
        edges.append(edge)
        at += count
    breadth, channels = srcs[0].shape[1:]
    wide = breadth + 8
    rows = ROWS * len(spans)
    square = pltpu.VMEM((channels, channels), jnp.bfloat16)
    return pl.pallas_call(
        functools.partial(window_kernel, tuple(spans), tuple(plan)),
        out_shape=jax.ShapeDtypeStruct((rows * breadth, channels), jnp.bfloat16),
        in_specs=[pl.BlockSpec(memory_space=pltpu.SMEM), pl.BlockSpec(memory_space=pltpu.VMEM)]
        + [pl.BlockSpec(memory_space=pltpu.HBM)] * 4 + [pl.BlockSpec(memory_space=pl.ANY)] * (2 * len(srcs)),
        out_specs=pl.BlockSpec(memory_space=pltpu.VMEM),
        scratch_shapes=[
            pltpu.VMEM((at, breadth, channels), jnp.bfloat16),
            pltpu.VMEM((at, 8, channels), jnp.bfloat16),
            pltpu.VMEM((at, wide, channels), jnp.float32),
            pltpu.VMEM((rows, breadth, channels), jnp.bfloat16),
            pltpu.VMEM((at, wide, 2 * channels), jnp.float32),
            pltpu.VMEM((rows, breadth, channels), jnp.bfloat16),
            pltpu.VMEM((len(spans), ROWS * QC, SPAN * KC), jnp.float32),
            square, square, square, square,
            pltpu.SemaphoreType.DMA((4 + 2 * len(srcs),)),
        ],
        compiler_params=pltpu.CompilerParams(vmem_limit_bytes=60 << 20),
        cost_estimate=pl.CostEstimate(flops=14_000_000_000, transcendentals=0, bytes_accessed=4_000_000),
    )(place, gains, wq, wk, wv, wo, *srcs, *edges)


TILE = 16
PART = 64
RIM = 2
SIDE = 8
PIECE = 512

def gather_kernel(plan, n_arrays, piece_rows, *refs):
    place_ref, gains_ref, idx_hbm, w_hbm, qa_hbm, ta_hbm, wk_hbm, wv_hbm, wo_hbm = refs[:9]
    arrays = refs[9:9 + n_arrays]
    (joined_ref, normed_ref, top_ref, bottom_ref, edge_ref, table, res,
     idx_ref, w_ref, qa_ref, ta_ref, wk_ref, wv_ref, wo_ref, stage, sems, stage_sems) = refs[9 + n_arrays:]
    copies = [
        pltpu.make_async_copy(src, dst, sems.at[n])
        for n, (src, dst) in enumerate((
            (idx_hbm, idx_ref), (w_hbm, w_ref), (wk_hbm, wk_ref), (wv_hbm, wv_ref), (qa_hbm, qa_ref), (ta_hbm, ta_ref), (wo_hbm, wo_ref)))
    ]
    for c in copies:
        c.start()
    height, breadth, channels = ta_ref.shape
    tiles = breadth // TILE
    rows = TILE * TILE
    total = height * breadth
    lanes = channels // 128

    slots = stage.shape[0]

    def copy(n):
        which, first = plan[n]
        return pltpu.make_async_copy(arrays[which].at[pl.ds(first, piece_rows)], stage.at[n % slots], stage_sems.at[n % slots])

    for n in range(slots):
        copy(n).start()
    for n in range(len(plan)):
        copy(n).wait()
        x = stage[n % slots].astype(jnp.float32)
        for j in range(lanes):
            table[pl.ds(n * (piece_rows // 8), piece_rows // 8), j] = x[:, 128 * j:128 * j + 128].reshape(piece_rows // 8, 8, 128)
        if n + slots < len(plan):
            copy(n + slots).start()
    flat = table.reshape(table.shape[0] * lanes * 8, 128)
    out = res.reshape(res.shape[0] * lanes * 8, 128)

    for c in copies[:2]:
        c.wait()

    idx1, w1 = idx_ref.reshape(4 * total), w_ref.reshape(4 * total)

    def line(tile, i):
        at0 = tile * (rows * lanes) + i * (TILE * lanes)
        base = i * breadth + tile * TILE
        for j in range(TILE):
            acc = None
            for k in range(4):
                at = base + (k * total + j)
                term = w1[at] * flat[pl.ds(idx1[at], lanes, stride=8), :]
                acc = term if acc is None else acc + term
            out[pl.ds(at0 + (j // 8) * (8 * lanes) + j % 8, lanes, stride=8), :] = acc

    def first_tile(i, carry):
        line(0, i)
        return carry

    lax.fori_loop(0, TILE, first_tile, 0)
    for c in copies[2:]:
        c.wait()

    def attend(t, carry):
        r = jnp.concatenate([res[pl.ds(t * (rows // 8), rows // 8), j].reshape(rows, 128) for j in range(lanes)], axis=1)
        nr = rms_rows(r.astype(jnp.bfloat16).astype(jnp.float32), gains_ref[2:3, :]).astype(jnp.bfloat16)
        kk = jnp.dot(nr, wk_ref[...], preferred_element_type=jnp.float32).astype(jnp.bfloat16)
        vv = jnp.dot(nr, wv_ref[...], preferred_element_type=jnp.float32).astype(jnp.bfloat16)
        qa = qa_ref[:, pl.ds(pl.multiple_of(t * TILE, TILE), TILE), :].reshape(rows, channels)
        following = jnp.minimum(t + 1, tiles - 1)
        units = [(l0, l1, q0) for l0, l1 in ((0, 256), (256, 384)) for q0 in range(0, rows, PART)]
        per = TILE // len(units)
        parts = {}
        for n, (l0, l1, q0) in enumerate(units):
            parts[l0, q0] = attend_heads(qa[q0:q0 + PART, l0:l1], kk[:, l0:l1], vv[:, l0:l1], None).astype(jnp.bfloat16)
            for i in range(n * per, n * per + per):
                line(following, i)
        mix = jnp.concatenate(
            [jnp.concatenate([parts[l0, q0] for l0 in (0, 256)], axis=1) for q0 in range(0, rows, PART)], axis=0)
        o = jnp.dot(mix, wo_ref[...], preferred_element_type=jnp.float32)
        cols = pl.ds(pl.multiple_of(t * TILE, TILE), TILE)
        joined = (ta_ref[:, cols, :].reshape(rows, channels).astype(jnp.float32) + o).astype(jnp.bfloat16)
        joined_ref[:, cols, :] = joined.reshape(TILE, TILE, channels)
        normed_ref[:, cols, :] = rms_rows(joined.astype(jnp.float32), gains_ref[3:4, :]).astype(jnp.bfloat16).reshape(TILE, TILE, channels)
        return carry

    lax.fori_loop(0, tiles, attend, 0)

    top_ref[...] = normed_ref[0:RIM]
    bottom_ref[...] = normed_ref[height - RIM:height]
    first_group = place_ref[1] == 0
    edge_ref[...] = jnp.where(first_group, normed_ref[:, breadth - SIDE:, :], normed_ref[:, 0:SIDE, :])

def gather_call(idx, weights, place, qa, ta, gains, wk, wv, wo, pieces):
    height, breadth, channels = ta.shape
    arrays, plan = [], []
    for rows, first in pieces:
        which = [n for n, array in enumerate(arrays) if array is rows]
        plan.append((which[0] if which else len(arrays), first))
        arrays += [] if which else [rows]
    piece_rows = PIECE
    n = len(pieces)
    total = height * breadth
    lanes = channels // 128
    assert height == TILE and channels == 384
    sm = pl.BlockSpec(memory_space=pltpu.SMEM)
    anywhere = pl.BlockSpec(memory_space=pl.ANY)
    square = pltpu.VMEM((channels, channels), jnp.bfloat16)
    vm = pl.BlockSpec(memory_space=pltpu.VMEM)
    shape = jax.ShapeDtypeStruct((height, breadth, channels), jnp.bfloat16)
    rim = jax.ShapeDtypeStruct((RIM, breadth, channels), jnp.bfloat16)
    return pl.pallas_call(
        functools.partial(gather_kernel, tuple(plan), len(arrays), piece_rows),
        out_shape=(shape, shape, rim, rim, jax.ShapeDtypeStruct((height, SIDE, channels), jnp.bfloat16)),
        in_specs=[sm, vm] + [anywhere] * 3 + [pl.BlockSpec(memory_space=pltpu.HBM)] * 4 + [anywhere] * len(arrays),
        out_specs=(vm,) * 5,
        scratch_shapes=[
            pltpu.VMEM((n * piece_rows // 8, lanes, 8, 128), jnp.float32),
            pltpu.VMEM((total // 8, lanes, 8, 128), jnp.float32),
            pltpu.SMEM(idx.shape, jnp.int32),
            pltpu.SMEM(idx.shape, jnp.float32),
            pltpu.VMEM(ta.shape, jnp.bfloat16),
            pltpu.VMEM(ta.shape, jnp.bfloat16),
            square, square, square,
            pltpu.VMEM((n, piece_rows, channels), jnp.bfloat16),
            pltpu.SemaphoreType.DMA((7,)),
            pltpu.SemaphoreType.DMA((n,)),
        ],
        compiler_params=pltpu.CompilerParams(vmem_limit_bytes=60 << 20),
        cost_estimate=pl.CostEstimate(flops=30_000_000_000, transcendentals=0, bytes_accessed=10_000_000),
    )(place, gains, idx, weights, qa, ta, wk, wv, wo, *arrays)


STEP1, STEP2 = 7, 6

def gelu(x):
    return 0.5 * x * (1.0 + jnp.tanh(0.7978845608028654 * (x + 0.044715 * (x * x * x))))

def tap_copies(src, dst, sems):
    channels = src.shape[-1]
    return [
        pltpu.make_async_copy(
            src.at[a, b], dst.at[pl.ds(a * channels, channels), pl.ds(b * channels, channels)], sems.at[3 * a + b])
        for a in range(3) for b in range(3)
    ]

def conv_rows(src, rows, count, w_ref):
    span, channels = src.shape[1], src.shape[2]
    lhs = [jnp.concatenate([src[pl.ds(row + a, count)] for a in range(3)], axis=-1) for row in rows]
    lhs = lhs[0] if len(lhs) == 1 else jnp.concatenate(lhs, axis=0)
    n = len(rows) * count * span
    y = jnp.dot(lhs.reshape(n, 3 * channels), w_ref[...], preferred_element_type=jnp.float32)
    return (pltpu.roll(y[:, :channels], 1, 0) + y[:, channels:2 * channels]
            + pltpu.roll(y[:, 2 * channels:], n - 1, 0)).reshape(len(rows) * count, span, channels)

def place_sides(field, rows, edge, place_ref, breadth):
    zero = jnp.zeros_like(edge)
    field[rows, 0:SIDE, :] = jnp.where(place_ref[1] > 0, edge, zero)
    field[rows, SIDE + breadth:, :] = jnp.where(place_ref[1] + breadth < place_ref[3], edge, zero)

def columns_inside(place_ref, span):
    col = lax.broadcasted_iota(jnp.int32, (1, span, 1), 1) + (place_ref[1] - SIDE)
    return (col >= 0) & (col < place_ref[3])

def first_kernel(step, place_ref, nc_ref, side_ref, w_hbm, inner_ref, field, w, sems):
    height, breadth, channels = nc_ref.shape
    span = field.shape[1]
    copies = tap_copies(w_hbm, w, sems)
    for c in copies:
        c.start()
    field[:, SIDE:SIDE + breadth, :] = nc_ref[...]
    place_sides(field, slice(0, height), side_ref[...], place_ref, breadth)
    ok = columns_inside(place_ref, span)
    for c in copies:
        c.wait()

    def rows(n, carry):
        x = gelu(conv_rows(field, (n * step,), step, w))
        inner_ref[pl.ds(n * step, step)] = jnp.where(ok, x, 0.0).astype(jnp.bfloat16)
        return carry

    lax.fori_loop(0, (height - 2) // step, rows, 0)

def second_kernel(step, inner_ref, joined_ref, w_hbm, out_ref, w, sems):
    height, breadth, channels = joined_ref.shape
    copies = tap_copies(w_hbm, w, sems)
    for c in copies:
        c.start()
    for c in copies:
        c.wait()

    def rows(n, carry):
        y = conv_rows(inner_ref, (n * step,), step, w)[:, SIDE:SIDE + breadth, :]
        at = pl.ds(n * step + RIM, step)
        out_ref[at] = (joined_ref[at].astype(jnp.float32) + y).astype(jnp.bfloat16)
        return carry

    lax.fori_loop(0, (height - 2 * RIM) // step, rows, 0)

def rim_kernel(place_ref, nc_ref, side_ref, top_ref, bottom_ref, side_rim_ref, inner_ref, joined_ref,
               w1_hbm, w2_hbm, merged_hbm, out_hbm, field, inner, done, w1, w2, sems1, sems2, out_sems):
    height, breadth, channels = joined_ref.shape
    span = field.shape[1]
    copies1, copies2 = tap_copies(w1_hbm, w1, sems1), tap_copies(w2_hbm, w2, sems2)
    for c in copies1 + copies2:
        c.start()
    ok = columns_inside(place_ref, span)
    for c in copies1:
        c.wait()
    for end in range(2):
        own = 0 if end == 0 else height - RIM
        at = 2 * RIM * end
        own_at, far_at = (at + RIM, at) if end == 0 else (at, at + RIM)
        far = top_ref if end == 0 else bottom_ref
        field[own_at:own_at + RIM, SIDE:SIDE + breadth, :] = nc_ref[own:own + RIM]
        place_sides(field, slice(own_at, own_at + RIM), side_ref[own:own + RIM], place_ref, breadth)
        field[far_at:far_at + RIM, SIDE:SIDE + breadth, :] = far[...]
        place_sides(field, slice(far_at, far_at + RIM), side_rim_ref[end * RIM:end * RIM + RIM], place_ref, breadth)
    x = gelu(conv_rows(field, (0, 2 * RIM), RIM, w1))
    n = lax.broadcasted_iota(jnp.int32, (2 * RIM, 1, 1), 0)
    row = place_ref[0] + n + jnp.where(n < RIM, -1, height - 1 - RIM)
    x = jnp.where((row >= 0) & (row < place_ref[2]) & ok, x, 0.0).astype(jnp.bfloat16)
    inner[0:RIM] = x[:RIM]
    inner[RIM:2 * RIM] = inner_ref[0:RIM]
    inner[2 * RIM:3 * RIM] = inner_ref[height - 2 - RIM:height - 2]
    inner[3 * RIM:4 * RIM] = x[RIM:]
    for c in copies2:
        c.wait()
    y = conv_rows(inner, (0, 2 * RIM), RIM, w2)[:, SIDE:SIDE + breadth, :]
    stores = []
    for end in range(2):
        own = 0 if end == 0 else height - RIM
        done[end] = (joined_ref[own:own + RIM].astype(jnp.float32) + y[end * RIM:end * RIM + RIM]).astype(jnp.bfloat16)
        stores.append(pltpu.make_async_copy(done.at[end], out_hbm.at[pl.ds(own, RIM)], out_sems.at[end]))
        stores[end].start()
    for c in stores:
        c.wait()

SM = pl.BlockSpec(memory_space=pltpu.SMEM)
VM = pl.BlockSpec(memory_space=pltpu.VMEM)
HB = pl.BlockSpec(memory_space=pl.ANY)

def first_call(place, nc, side, w1):
    height, breadth, channels = nc.shape
    span = breadth + 2 * SIDE
    return pl.pallas_call(
        functools.partial(first_kernel, STEP1),
        out_shape=jax.ShapeDtypeStruct((height - 2, span, channels), jnp.bfloat16),
        in_specs=[SM, VM, VM, HB],
        out_specs=VM,
        scratch_shapes=[
            pltpu.VMEM((height, span, channels), jnp.bfloat16),
            pltpu.VMEM((3 * channels, 3 * channels), jnp.bfloat16),
            pltpu.SemaphoreType.DMA((9,)),
        ],
        compiler_params=pltpu.CompilerParams(vmem_limit_bytes=40 << 20),
        cost_estimate=pl.CostEstimate(flops=10_000_000_000, transcendentals=0, bytes_accessed=4_000_000),
    )(place, nc, side, w1)

def second_call(inner, joined, w2):
    channels = joined.shape[-1]
    return pl.pallas_call(
        functools.partial(second_kernel, STEP2),
        out_shape=jax.ShapeDtypeStruct(joined.shape, jnp.bfloat16),
        in_specs=[VM, VM, HB],
        out_specs=VM,
        scratch_shapes=[pltpu.VMEM((3 * channels, 3 * channels), jnp.bfloat16), pltpu.SemaphoreType.DMA((9,))],
        compiler_params=pltpu.CompilerParams(vmem_limit_bytes=40 << 20),
        cost_estimate=pl.CostEstimate(flops=8_000_000_000, transcendentals=0, bytes_accessed=4_000_000),
    )(inner, joined, w2)

def rim_call(place, nc, side, top, bottom, side_rim, inner, joined, w1, w2, merged):
    height, breadth, channels = nc.shape
    span = breadth + 2 * SIDE
    return pl.pallas_call(
        rim_kernel,
        out_shape=jax.ShapeDtypeStruct(joined.shape, jnp.bfloat16),
        in_specs=[SM] + [VM] * 7 + [HB] * 3,
        out_specs=HB,
        input_output_aliases={10: 0},
        scratch_shapes=[
            pltpu.VMEM((4 * RIM, span, channels), jnp.bfloat16),
            pltpu.VMEM((4 * RIM, span, channels), jnp.bfloat16),
            pltpu.VMEM((2, RIM, breadth, channels), jnp.bfloat16),
            pltpu.VMEM((3 * channels, 3 * channels), jnp.bfloat16),
            pltpu.VMEM((3 * channels, 3 * channels), jnp.bfloat16),
            pltpu.SemaphoreType.DMA((9,)),
            pltpu.SemaphoreType.DMA((9,)),
            pltpu.SemaphoreType.DMA((2,)),
        ],
        compiler_params=pltpu.CompilerParams(vmem_limit_bytes=40 << 20),
        cost_estimate=pl.CostEstimate(flops=5_000_000_000, transcendentals=0, bytes_accessed=4_000_000),
    )(place, nc, side, top, bottom, side_rim, inner, joined, w1, w2, merged)

def pack_kernel(place_ref, rows_ref, count_ref, keep_ref, give_ref):
    swath, group, groups = place_ref[4], place_ref[5], place_ref[6]
    peers, cap = rows_ref.shape
    lines = cap // 128
    for step in range(3):
        near = jnp.clip(swath + step - 1, 0, peers // groups - 1) * groups
        for ref, at in ((keep_ref, near + group), (give_ref, near + 1 - group)):
            row = rows_ref[pl.ds(at, 1), :]
            for n in range(lines):
                ref[step, n:n + 1, :] = row[:, 128 * n:128 * n + 128]
            ref[step, lines:lines + 1, :] = jnp.full((1, 128), count_ref[0, at], jnp.int32)


def pack_call(place, rows, count):
    sm = pl.BlockSpec(memory_space=pltpu.SMEM)
    vm = pl.BlockSpec(memory_space=pltpu.VMEM)
    shape = jax.ShapeDtypeStruct((3, rows.shape[1] // 128 + 1, 128), jnp.int32)
    return pl.pallas_call(
        pack_kernel, out_shape=(shape, shape), in_specs=[sm, vm, sm], out_specs=(vm, vm),
        cost_estimate=pl.CostEstimate(flops=1_000_000, transcendentals=0, bytes_accessed=100_000),
    )(place, rows, count)


def index_kernel(place_ref, slots_ref, weights_ref, upper_ref, keep_ref, taken_ref, lower_ref, index_ref, live_ref):
    swath, group, groups, cap, block = (place_ref[n] for n in range(4, 9))
    lines = keep_ref.shape[1] - 1
    blocks = ((upper_ref, 0), (upper_ref, 1), (keep_ref, 1), (taken_ref, 1), (lower_ref, 0), (lower_ref, 1))
    slots = slots_ref[...]
    peer, place = lax.div(slots, cap), lax.rem(slots, cap)
    step = lax.div(peer, groups) - swath
    other = jnp.where(lax.rem(peer, groups) == group, 0, 1)
    source = (step + 1) * 2 + other
    line, lane = source * lines + lax.div(place, 128), lax.rem(place, 128)
    cell = jnp.zeros_like(slots)
    count = jnp.zeros_like(slots)
    for s, (ref, at) in enumerate(blocks):
        count = jnp.where(source == s, jnp.broadcast_to(ref[at, lines:lines + 1, :], slots.shape), count)
        for n in range(lines):
            row = jnp.broadcast_to(ref[at, n:n + 1, :], slots.shape)
            picked = jnp.take_along_axis(row, lane, axis=1)
            cell = jnp.where(line == s * lines + n, picked, cell)
    toward = jnp.where(lax.rem(swath, 2) == 0, 1, -1)
    slot = jnp.where(step == 0, 0, jnp.where(step == toward, 1, 2))
    row = (slot * 2 + other) * block + cell
    index_ref[...] = lax.div(row, 8) * (8 * 3) + lax.rem(row, 8)
    live_ref[...] = jnp.where(place < count, weights_ref[...], 0.0)


def index_call(place, slots, weights, tables):
    sm = pl.BlockSpec(memory_space=pltpu.SMEM)
    vm = pl.BlockSpec(memory_space=pltpu.VMEM)
    return pl.pallas_call(
        index_kernel,
        out_shape=(jax.ShapeDtypeStruct(slots.shape, jnp.int32), jax.ShapeDtypeStruct(slots.shape, jnp.float32)),
        in_specs=[sm] + [vm] * 6,
        out_specs=(vm, vm),
        cost_estimate=pl.CostEstimate(flops=1_000_000, transcendentals=0, bytes_accessed=100_000),
    )(place, slots, weights, *tables)


def query_kernel(tokens_ref, gains_ref, w_ref, out_ref):
    height, breadth, channels = tokens_ref.shape
    for r in range(0, height, 4):
        x = rms_rows(tokens_ref[r:r + 4].reshape(4 * breadth, channels).astype(jnp.float32), gains_ref[1:2, :]).astype(jnp.bfloat16)
        q = jnp.dot(x, w_ref[...], preferred_element_type=jnp.float32).astype(jnp.bfloat16)
        out_ref[r:r + 4] = (q * jnp.bfloat16(HD ** -0.5)).reshape(4, breadth, channels)


def query_call(tokens, gains, w):
    return pl.pallas_call(
        query_kernel,
        out_shape=jax.ShapeDtypeStruct(tokens.shape, jnp.bfloat16),
        in_specs=[VM] * 3,
        out_specs=VM,
        compiler_params=pltpu.CompilerParams(vmem_limit_bytes=32 << 20),
        cost_estimate=pl.CostEstimate(flops=1_000_000, transcendentals=0, bytes_accessed=4_000_000),
    )(tokens, gains, w)


def body(
    tokens_b,
    tokens_a,
    pack_rows,
    pack_count,
    gather_slots,
    blend_weights,
    swath_gain,
    swath_query,
    swath_key,
    swath_value,
    swath_out,
    query_gain,
    source_gain,
    cross_query,
    cross_key,
    cross_value,
    cross_out,
    conv_gain,
    conv_first,
    conv_second,
):
    height, breadth, channels = tokens_b.shape
    swaths, groups = lax.axis_size("swath"), lax.axis_size("group")
    swath, group = lax.axis_index("swath"), lax.axis_index("group")
    assert groups == 2 and swaths % 2 == 0
    whole = [height * swaths, breadth * groups]
    down = [(i, i + 1) for i in range(swaths - 1)]
    up = [(j, i) for i, j in down]
    swap = [(0, 1), (1, 0)]
    pairs = [(i, i ^ 1) for i in range(swaths)]
    relay = [(i, j) for i in range(swaths) for j in [i + 2 if i % 2 == 0 else i - 2] if 0 <= j < swaths]

    def inner_edge(field):
        start = (1 - group) * (breadth - SIDE)
        return lax.dynamic_slice_in_dim(field, start, SIDE, axis=1)

    def after(values, *results):
        return lax.optimization_barrier((values, *results))[0]

    cap = pack_rows.shape[-1]
    place = jnp.stack([
        swath * height, group * breadth, jnp.int32(whole[0]), jnp.int32(whole[1]),
        swath, group, jnp.int32(groups), jnp.int32(cap), jnp.int32(height * breadth),
    ]).astype(jnp.int32)

    margin = 3
    side = lax.ppermute(inner_edge(tokens_b), "group", swap)
    top = lax.ppermute(tokens_b[height - margin:], "swath", down)
    bottom = lax.ppermute(tokens_b[:margin], "swath", up)
    projections = (swath_query, swath_key, swath_value, swath_out)

    def near(rows):
        return lax.ppermute(rows, "swath", pairs)

    def far(rows):
        return lax.ppermute(rows, "swath", relay)

    r0, r1, r2, r3 = range(0, height, ROWS)
    middle = window_call(place, swath_gain, *projections, ((r1, 0), (r2, ROWS)), [(tokens_b, side, r1 - margin, r1 - margin, SPAN + ROWS)])
    near_middle = near(middle)
    row = lax.broadcasted_iota(jnp.int32, (8, channels), 0)
    gains = sum(jnp.where(row == n, gain[None, :], 0.0) for n, gain in enumerate((swath_gain, query_gain, source_gain, after(conv_gain, middle))))
    rims = after(jnp.concatenate([top, bottom], axis=0), middle)
    rims = lax.ppermute(inner_edge(rims), "group", swap)
    ends = window_call(
        after(place, middle), swath_gain, *projections, ((r0, 0), (r3, SPAN)),
        [(top, rims, 0, 0, margin), (tokens_b, side, 0, 0, SPAN - margin),
         (tokens_b, side, r3 - margin, r3 - margin, SPAN - margin), (bottom, rims, 0, margin, margin)],
    )
    near_ends = near(ends)

    pack_rows, pack_count = after((pack_rows, pack_count), near_ends)
    keep, give = pack_call(place, pack_rows.reshape(-1, cap), pack_count.reshape(1, -1))
    taken = lax.ppermute(give, "group", swap)
    upper = lax.ppermute(jnp.concatenate([keep[2:], taken[2:]], axis=0), "swath", down)
    lower = lax.ppermute(jnp.concatenate([keep[:1], taken[:1]], axis=0), "swath", up)
    tokens_a = after(tokens_a, ends)
    index, live = index_call(
        place, gather_slots.reshape(-1, 128), blend_weights.reshape(-1, 128), (upper, keep, taken, lower)
    )
    query_a = query_call(tokens_a, gains, cross_query)

    far_middle = far(near_middle)
    near_ends, query_a = lax.optimization_barrier((near_ends, query_a))
    far_ends = far(near_ends)
    swapped = lambda rows: lax.ppermute(rows, "group", swap)
    blocks = [(middle, ends), (swapped(middle), swapped(ends)), (near_middle, near_ends)]
    blocks += [(swapped(near_middle), swapped(after(near_ends, index, live)))]
    others = (swapped(after(far_middle, index, live)), swapped(far_ends))
    blocks += [(far_middle, far_ends), others]
    size = ROWS * breadth
    pieces = [piece for m, e in blocks for piece in ((e, 0), (m, 0), (m, size), (e, size))]
    joined, normed_c, first_rows, last_rows, edge = gather_call(
        index, live, place, query_a, tokens_a, gains,
        cross_key, cross_value, cross_out, pieces,
    )

    side = lax.ppermute(edge, "group", swap)
    top = lax.ppermute(last_rows, "swath", down)
    bottom = lax.ppermute(first_rows, "swath", up)
    inner = first_call(place, normed_c, side, conv_first)
    rims = after(jnp.concatenate([top, bottom], axis=0), inner)
    rims = lax.ppermute(inner_edge(rims), "group", swap)
    merged = second_call(inner, joined, conv_second)
    return rim_call(place, normed_c, side, top, bottom, rims, inner, joined, conv_first, conv_second, merged)


def solution(mesh):
    rows = P(("strip", "swath"), "group", None)
    maps = P(None, ("strip", "swath"), "group")
    placed = (rows, rows, P(("strip", "swath"), "group", None, None), rows, maps, maps) + (P(),) * 14
    return jax.shard_map(body, mesh=mesh, in_specs=placed, out_specs=rows, check_vma=False)
```
